32 devices in a mesh: seq: 16 (over z, y, x), pair: 2 (over core).
Axes of the slice: x: 2, y: 2, z: 4, core: 2. Of those that a mesh axis runs over, the one named last changes fastest.
Arguments:
- tokens_in: bfloat16 [4096, 1024], P(('seq', 'pair')), may hold values from -6 to 6
- queries: bfloat16 [4096, 1024], P(('seq', 'pair')), may hold values from -500 to 500
- key_value: bfloat16 [4096, 128], P(('seq', 'pair')), may hold values from -6 to 6
- out_grad: bfloat16 [4096, 1024], P(('seq', 'pair')), may hold values from -4 to 4
- cluster_of: int32 [4096, 16], P(('seq', 'pair')), may hold values from 0 to 127, as said below
- slot_of: int32 [4096, 16], P(('seq', 'pair')), may hold values from 0 to 1023, as said below
Outputs:
- weight_grad: float32 [1024, 1024], P(('seq', 'pair'))
The draws below stay inside these ranges and needn't reach their ends.
Inputs may be any that keep to these rules, and one draw needn't show every extreme that they name: `cluster_of`: cluster c belongs to owner group c // 8. Of the 2048 rows of one aligned block of 128 tokens, at most 256 name clusters of one owner group; in every draw some owner group receives exactly 256 rows from every block of even index and some from every block of odd index. No two rows share a cluster and a slot. Rows of the k-th aligned block of 128 tokens take slots of half k % 2, that is slot_of // 512 == k % 2. Half of all slots have a member in all; single clusters hold more or fewer.
All inputs are finite; a program needn't handle non-finite values.
Results may differ from the reference program's by a relative error of at most 0.0041.
Values may be sent and summed in bfloat16 or wider, within the bound.
No kernel may reach another device: no remote copies, remote signals or barrier semaphores. Data moves between devices by JAX's collectives and lax.ppermute only.
A program may use at most 64 MiB of HBM per device.

```python
import jax
import jax.numpy as jnp
from jax import lax

D = 1024
H = 16
HD = 64
CAP = 1024
TOK_DEV = 128
HALF = 512
CL_DEV = 8
GROUPS = 16
BOUND = 256
TOKENS = 4096
CLUSTERS = 128


def assign_rows(key):
    base_key = jax.random.fold_in(key, 17)
    split_keys = jax.random.split(base_key, 5)
    row_count = TOK_DEV * H
    device_count = 2 * GROUPS
    cell_count = GROUPS * BOUND
    starred = jax.random.randint(split_keys[0], (2,), 0, GROUPS)
    levels = jax.random.randint(split_keys[1], (2, GROUPS), 0, 4) * 256
    biases = levels + 4096 * (jnp.arange(GROUPS)[None, :] == starred[:, None]).astype(jnp.int32)
    noises = jax.random.randint(split_keys[2], (device_count, GROUPS, BOUND), 0, 256)
    parity = jnp.arange(device_count) % 2
    ranking = (biases[parity][:, :, None] + noises).reshape(device_count, cell_count)
    ranking = ranking * cell_count + jnp.arange(cell_count)[None, :]
    chosen = lax.top_k(ranking, row_count)[1]
    row_keys = jax.random.split(split_keys[3], device_count)
    shuffle = jax.vmap(lambda each: jax.random.permutation(each, row_count))(row_keys)
    chosen = jnp.take_along_axis(chosen, shuffle, axis=1)
    owners = chosen // BOUND
    within = chosen % BOUND
    sources = jnp.arange(device_count) // 2
    slot_keys = jax.random.split(split_keys[4], GROUPS * 2)
    tables = jax.vmap(lambda each: jax.random.permutation(each, cell_count))(slot_keys).reshape(GROUPS, 2, cell_count)
    local_slot = tables[owners, parity[:, None], sources[:, None] * BOUND + within]
    clusters = owners * CL_DEV + local_slot // HALF
    slots = parity[:, None] * HALF + local_slot % HALF
    return (clusters.reshape(TOKENS, H).astype(jnp.int32), slots.reshape(TOKENS, H).astype(jnp.int32))


def draw_cluster_of(key, part):
    return assign_rows(key)[0]


def draw_slot_of(key, part):
    return assign_rows(key)[1]


def draw_queries(key, part):
    base = jax.random.normal(jax.random.fold_in(key, 3), (TOKENS, H, HD), jnp.float32)
    values = jnp.clip(base, -6.0, 6.0)
    return values.reshape(TOKENS, H * HD).astype(jnp.bfloat16)


def with_spikes(entries, key, source, target, blocks, factor):
    owner, partner = [(jnp.arange(entries.shape[axis_at]) // (entries.shape[axis_at] // blocks)).reshape([-1 if axis == axis_at else 1 for axis in range(entries.ndim)]) for axis_at in (source, target)]
    chosen = jax.random.permutation(key, blocks)[partner]
    strong = (owner == chosen) | (owner == (partner + blocks // 2) % blocks)
    return jnp.where(strong, factor * entries, entries)


def block_levels(rng, shape, shards, smallest, top_value):
    def one(dim, shards_of):
        draws = jax.random.uniform(jax.random.fold_in(jax.random.fold_in(rng, 6), dim), (shards_of,), jnp.float32, smallest / len(shards), top_value / len(shards))
        return jnp.repeat(jnp.exp(draws), shape[dim] // shards_of).reshape((-1,) + (1,) * (len(shape) - dim - 1))

    factor_of = one(*shards[0])
    for cut in shards[1:]:
        factor_of = factor_of * one(*cut)
    return factor_of


def gaussian(own_key, extent, scale, limit, cuts=(), kind=jnp.bfloat16):
    drawn = scale * jax.random.normal(own_key, extent, jnp.float32)
    if cuts:
        drawn = drawn * block_levels(own_key, extent, cuts, -0.22, 0.18)
    return jnp.clip(drawn, -limit, limit).astype(kind)


def gaussian_with(stream_key, dims, width, bound, shards, heavy, held_as=jnp.bfloat16):
    drawn = width * jax.random.normal(stream_key, dims, jnp.float32)
    if shards:
        drawn = drawn * block_levels(stream_key, dims, shards, -0.22, 0.18)
    return jnp.clip(with_spikes(drawn, jax.random.fold_in(stream_key, 3), *heavy), -bound, bound).astype(held_as)


def setup_inputs(seed: int = 0) -> dict:
    key_of = jax.random.split(jax.random.key(seed), 7)
    tokens_in = gaussian_with(key_of[0], (TOKENS, D), 1.0, 6.0, ((0, 32),), (0, 1, 32, 2.75))
    queries = draw_queries(jax.random.fold_in(key_of[6], 71), 0)
    key_value = gaussian(key_of[2], (TOKENS, 2 * HD), 1.0, 6.0, ((0, 32),))
    out_grad = gaussian(key_of[3], (TOKENS, H * HD), (16.0 / TOKENS ** 0.5), 4.0, ((0, 32),))
    cluster_of = draw_cluster_of(jax.random.fold_in(key_of[6], 71), 0)
    slot_of = draw_slot_of(jax.random.fold_in(key_of[6], 71), 0)
    return {"tokens_in": tokens_in, "queries": queries, "key_value": key_value, "out_grad": out_grad, "cluster_of": cluster_of, "slot_of": slot_of}


def cluster_grad(query_part, key_part, live_keys):
    score_scale = HD ** (-0.5)
    query_rows = query_part[:, :HD]
    grad_rows = query_part[:, HD:]
    key_rows = key_part[:, :HD]
    value_rows = key_part[:, HD:]
    scores = jnp.dot(query_rows, key_rows.T, preferred_element_type=jnp.float32) * score_scale
    scores = jnp.where(live_keys[None, :] > 0, scores, jnp.float32(-1e+30))
    row_max = lax.optimization_barrier(jnp.max(scores, axis=1, keepdims=True))
    weights = jnp.exp(scores - row_max)
    probs = weights / lax.optimization_barrier(jnp.sum(weights, axis=1, keepdims=True))
    prob_grad = jnp.dot(grad_rows, value_rows.T, preferred_element_type=jnp.float32)
    row_dot = lax.optimization_barrier(jnp.sum(probs * prob_grad, axis=1, keepdims=True))
    score_grad = (probs * (prob_grad - row_dot) * score_scale).astype(jnp.bfloat16)
    return jnp.dot(score_grad, key_rows, preferred_element_type=jnp.float32).astype(jnp.bfloat16)

def reference(tokens_in, queries, key_value, out_grad, cluster_of, slot_of):
    row_count = TOKENS * H
    flat_place = (cluster_of * CAP + slot_of).reshape(row_count).astype(jnp.int32)
    members = jnp.full((CLUSTERS * CAP,), -1, jnp.int32).at[flat_place].set(jnp.arange(row_count, dtype=jnp.int32))
    paired_rows = jnp.concatenate([queries.reshape(row_count, HD), out_grad.reshape(row_count, HD)], axis=1)

    def one_cluster(cluster):
        member_rows = lax.dynamic_slice_in_dim(members, (cluster * CAP).astype(jnp.int32), CAP)
        present = member_rows >= 0
        safe_rows = jnp.where(present, member_rows, 0)
        query_part = jnp.where(present[:, None], paired_rows[safe_rows], jnp.zeros((), paired_rows.dtype))
        key_part = jnp.where(present[:, None], key_value[safe_rows // H], jnp.zeros((), key_value.dtype))
        return cluster_grad(query_part, key_part, present.astype(jnp.float32))
    cluster_grads = lax.map(one_cluster, jnp.arange(CLUSTERS, dtype=jnp.int32))
    query_grad = cluster_grads.reshape(CLUSTERS * CAP, HD)[flat_place].reshape(TOKENS, H * HD)
    return jnp.dot(tokens_in.T, query_grad, preferred_element_type=jnp.float32)
```

```python
import jax
import jax.numpy as jnp
from jax import lax
from jax.experimental import pallas as pl
from jax.experimental.pallas import tpu as pltpu
from jax.sharding import PartitionSpec as P

H = 16
HD = 64
HALF = 512
CL_DEV = 8
SCALE = HD ** (-0.5)
LOG2E = 1.4426950408889634
TILE = 512


def attend_kernel(q_ref, g_ref, cl_ref, *refs):
    kv_refs = refs[:-6]
    out_ref, rhs, val, key, sc, pg = refs[-6:]
    pair = pl.program_id(0)
    tok = q_ref.shape[0]
    lanes = 2 * HD
    clusters = (rhs.shape[0] - lanes) // 2
    total = rhs.shape[1]
    tiles = total // TILE

    @pl.when(pair == 0)
    def _():
        ids = lax.broadcasted_iota(jnp.int32, (clusters, tok), 0).astype(jnp.float32)
        at = 0
        for kv_ref in kv_refs:
            for j in range(kv_ref.shape[0]):
                cols = pl.ds(at, tok)
                kt = kv_ref[j, 0:HD, :]
                vt = kv_ref[j, HD : 2 * HD, :]
                cl = kv_ref[j, 2 * HD : 2 * HD + H, :].astype(jnp.float32)
                rhs[0:HD, cols] = kt
                rhs[HD : 2 * HD, cols] = kt
                val[0:HD, cols] = vt
                val[HD : 2 * HD, cols] = vt
                k2 = jnp.concatenate([kt, kt], axis=0).astype(jnp.float32)
                key[cols, :] = k2.T.astype(jnp.bfloat16)
                count = jnp.zeros((clusters, tok), jnp.float32)
                for h in range(H):
                    count += jnp.where(cl[h : h + 1, :] == ids, 1.0, 0.0)
                bias = jnp.where(
                    count > 0.0, jnp.log(jnp.maximum(count, 1.0)) * (1.0 / SCALE), -1e30
                )
                hi = bias.astype(jnp.bfloat16)
                lo = bias - hi.astype(jnp.float32)
                lo = jnp.where(count > 0.0, lo, 0.0).astype(jnp.bfloat16)
                rhs[lanes : lanes + clusters, cols] = hi
                rhs[lanes + clusters :, cols] = lo
                at += tok

    lane = lax.broadcasted_iota(jnp.int32, (tok, lanes), 1)
    low = lane < HD
    q2 = q_ref[...]
    g2 = g_ref[...]
    zero = jnp.zeros_like(q2)
    head = lax.broadcasted_iota(jnp.int32, (tok, H), 1)
    own = lax.broadcasted_iota(jnp.int32, (tok, clusters), 1)
    lhs = []
    for odd in range(2):
        mine = jnp.sum(jnp.where(head == 2 * pair + odd, cl_ref[...], 0), axis=1, keepdims=True)
        hot = jnp.where(own == mine, 1.0, 0.0).astype(jnp.bfloat16)
        part = jnp.where(low, q2, zero) if odd == 0 else jnp.where(low, zero, q2)
        lhs.append(jnp.concatenate([part, hot, hot], axis=1))
    lhs = jnp.concatenate(lhs, axis=0)
    grads = jnp.concatenate([jnp.where(low, g2, zero), jnp.where(low, zero, g2)], axis=0)
    rows = 2 * tok

    top = jnp.full((rows, lanes), -3e38, jnp.float32)
    for t in range(tiles):
        cols = slice(t * TILE, (t + 1) * TILE)
        s = jnp.dot(lhs, rhs[:, cols], preferred_element_type=jnp.float32)
        sc[:, cols] = s
        for b in range(TILE // lanes):
            top = jnp.maximum(top, s[:, b * lanes : (b + 1) * lanes])
    top = jnp.max(top, axis=1, keepdims=True)

    denom = jnp.zeros((rows, lanes), jnp.float32)
    dots = jnp.zeros((rows, lanes), jnp.float32)
    for t in range(tiles):
        cols = slice(t * TILE, (t + 1) * TILE)
        w = jnp.exp2((sc[:, cols] - top) * (SCALE * LOG2E))
        sc[:, cols] = w
        p = jnp.dot(grads, val[:, cols], preferred_element_type=jnp.float32)
        pg[:, cols] = p
        wp = w * p
        for b in range(TILE // lanes):
            denom += w[:, b * lanes : (b + 1) * lanes]
            dots += wp[:, b * lanes : (b + 1) * lanes]
    denom = jnp.sum(denom, axis=1, keepdims=True)
    inv = SCALE / denom
    dot = jnp.sum(dots, axis=1, keepdims=True) / denom

    acc = jnp.zeros((rows, lanes), jnp.float32)
    for t in range(tiles):
        cols = slice(t * TILE, (t + 1) * TILE)
        ds = ((sc[:, cols] * inv) * (pg[:, cols] - dot)).astype(jnp.bfloat16)
        acc += jnp.dot(ds, key[cols, :], preferred_element_type=jnp.float32)
    out_ref[...] = jnp.where(low, acc[:tok], acc[tok:]).astype(jnp.bfloat16)


def attend(queries, out_grad, cluster_of, gathered, clusters):
    tok, width = queries.shape
    total = sum(g.shape[0] for g in gathered) * tok
    lanes = 2 * HD
    specs = [
        pl.BlockSpec((tok, lanes), lambda i: (0, i)),
        pl.BlockSpec((tok, lanes), lambda i: (0, i)),
        pl.BlockSpec((tok, H), lambda i: (0, 0)),
    ] + [pl.BlockSpec(g.shape, lambda i: (0, 0, 0)) for g in gathered]
    return pl.pallas_call(
        attend_kernel,
        grid=(width // lanes,),
        in_specs=specs,
        out_specs=pl.BlockSpec((tok, lanes), lambda i: (0, i)),
        out_shape=jax.ShapeDtypeStruct((tok, width), jnp.bfloat16),
        scratch_shapes=[
            pltpu.VMEM((lanes + 2 * clusters, total), jnp.bfloat16),
            pltpu.VMEM((lanes, total), jnp.bfloat16),
            pltpu.VMEM((total, lanes), jnp.bfloat16),
            pltpu.VMEM((2 * tok, total), jnp.float32),
            pltpu.VMEM((2 * tok, total), jnp.float32),
        ],
        compiler_params=pltpu.CompilerParams(vmem_limit_bytes=40 * 1024 * 1024),
    )(queries, out_grad, cluster_of, *gathered)


def xor_permute(x, axis, mask):
    n = lax.axis_size(axis)
    return lax.ppermute(x, axis, [(i, i ^ mask) for i in range(n)])


def dense(tokens_in, queries, key_value, out_grad, cluster_of, slot_of):
    n = lax.axis_size("seq")
    tok, width = queries.shape
    me = lax.axis_index("pair")
    low = 1
    while low * low < n:
        low *= 2
    high = n // low
    own = jnp.concatenate([key_value.T, cluster_of.T.astype(jnp.bfloat16)], axis=0)[None]
    column = jnp.concatenate([own] + [xor_permute(own, "seq", low * k) for k in range(1, high)])
    parts = [column] + [xor_permute(column, "seq", k) for k in range(1, low)]
    parts = parts + [xor_permute(p, "pair", 1) for p in parts]

    depth = tokens_in.shape[1]
    x4 = tokens_in.reshape(tok, n, 2, depth // (2 * n))
    x_mine = lax.dynamic_index_in_dim(x4, me, 2, keepdims=False).reshape(tok, depth // 2)
    x_other = lax.dynamic_index_in_dim(x4, 1 - me, 2, keepdims=False).reshape(tok, depth // 2)
    x_got = xor_permute(x_other, "pair", 1)

    mine = attend(queries, out_grad, cluster_of, parts, n * CL_DEV)
    other = xor_permute(mine, "pair", 1)
    contract = (((0,), (0,)), ((), ()))
    block = lax.dot_general(
        x_mine, mine, contract, preferred_element_type=jnp.float32
    ) + lax.dot_general(x_got, other, contract, preferred_element_type=jnp.float32)
    block = block.astype(jnp.bfloat16).reshape(n, depth // (2 * n), width)
    got = lax.all_to_all(block, "seq", 0, 0, tiled=True)
    return jnp.sum(got.astype(jnp.float32), axis=0)


def cluster_grad(query_part, key_part, live_keys):
    query_rows = query_part[:, :HD]
    grad_rows = query_part[:, HD:]
    key_rows = key_part[:, :HD]
    value_rows = key_part[:, HD:]
    scores = jnp.dot(query_rows, key_rows.T, preferred_element_type=jnp.float32) * SCALE
    scores = jnp.where(live_keys[None, :] > 0, scores, jnp.float32(-1e30))
    row_max = jnp.max(scores, axis=1, keepdims=True)
    weights = jnp.exp(scores - row_max)
    probs = weights / jnp.sum(weights, axis=1, keepdims=True)
    prob_grad = jnp.dot(grad_rows, value_rows.T, preferred_element_type=jnp.float32)
    row_dot = jnp.sum(probs * prob_grad, axis=1, keepdims=True)
    score_grad = (probs * (prob_grad - row_dot) * SCALE).astype(jnp.bfloat16)
    return jnp.dot(score_grad, key_rows, preferred_element_type=jnp.float32).astype(jnp.bfloat16)


def routed(tokens_in, queries, key_value, out_grad, cluster_of, slot_of):
    groups = lax.axis_size("seq")
    tok_count = queries.shape[0]
    row_count = tok_count * H
    bound_rows = 2 * row_count // groups
    slot_count = CL_DEV * HALF
    owners = (cluster_of // CL_DEV).reshape(row_count)
    local_slot = (cluster_of % CL_DEV * HALF + slot_of % HALF).reshape(row_count)
    picked = (owners[:, None] == jnp.arange(groups, dtype=jnp.int32)[None, :]).astype(jnp.int32)
    ranked = jnp.sum(jnp.cumsum(picked, axis=0) * picked, axis=1) - 1
    cell_index = owners * bound_rows + ranked
    paired_rows = jnp.concatenate(
        [queries.reshape(row_count, HD), out_grad.reshape(row_count, HD)], axis=1
    )
    packed = jnp.concatenate([paired_rows, jnp.repeat(key_value, H, axis=0)], axis=1)
    outgoing = jnp.zeros((groups * bound_rows, 4 * HD), jnp.bfloat16).at[cell_index].set(packed)
    labels = jnp.full((groups * bound_rows,), -1, jnp.int32).at[cell_index].set(local_slot)
    incoming = lax.all_to_all(
        outgoing.reshape(groups, bound_rows, 4 * HD), "seq", 0, 0, tiled=True
    )
    labels_in = lax.all_to_all(labels.reshape(groups, bound_rows), "seq", 0, 0, tiled=True)
    target = labels_in.reshape(groups * bound_rows)
    target_safe = jnp.where(target >= 0, target, slot_count)
    arranged = (
        jnp.zeros((slot_count, 4 * HD), jnp.bfloat16)
        .at[target_safe]
        .set(incoming.reshape(groups * bound_rows, 4 * HD), mode="drop")
    )
    live_slot = (
        jnp.zeros((slot_count,), jnp.bfloat16)
        .at[target_safe]
        .set(jnp.ones((groups * bound_rows,), jnp.bfloat16), mode="drop")
    )
    arranged = arranged.reshape(CL_DEV, HALF, 4 * HD)
    keys_all = lax.all_gather(arranged[:, :, 2 * HD :], "pair", axis=1, tiled=True)
    live_all = lax.all_gather(live_slot.reshape(CL_DEV, HALF), "pair", axis=1, tiled=True)
    cluster_grads = lax.map(
        lambda ops: cluster_grad(*ops), (arranged[:, :, : 2 * HD], keys_all, live_all)
    )
    slot_grads = cluster_grads.reshape(slot_count, HD)
    going_back = jnp.where(
        target[:, None] >= 0,
        slot_grads[jnp.minimum(target_safe, slot_count - 1)],
        jnp.zeros((), jnp.bfloat16),
    )
    returned = lax.all_to_all(
        going_back.reshape(groups, bound_rows // 2, 2 * HD), "seq", 0, 0, tiled=True
    )
    query_grad = returned.reshape(groups * bound_rows, HD)[cell_index].reshape(tok_count, H * HD)
    partial_rows = lax.psum_scatter(
        lax.dot_general(
            tokens_in, query_grad, (((0,), (0,)), ((), ())), preferred_element_type=jnp.float32
        ),
        "seq",
        scatter_dimension=0,
        tiled=True,
    )
    return lax.psum_scatter(partial_rows, "pair", scatter_dimension=0, tiled=True)


def solution(mesh):
    n = mesh.shape["seq"]
    small = n * CL_DEV <= 128 and n & (n - 1) == 0
    spec = P(("seq", "pair"), None)
    return jax.shard_map(
        dense if small else routed,
        mesh=mesh,
        in_specs=(spec,) * 6,
        out_specs=spec,
        check_vma=False,
    )
```

```python
import jax
import jax.numpy as jnp
from jax import lax
from jax.experimental import pallas as pl
from jax.experimental.pallas import tpu as pltpu
from jax.sharding import PartitionSpec as P

H = 16
HD = 64
HALF = 512
CL_DEV = 8
SCALE = HD ** (-0.5)
LOG2E = 1.4426950408889634
TILE = 512


def prepare_rows_kernel(q_ref, g_ref, cl_ref, lhs, grd):
    tok, width = q_ref.shape
    lanes = 2 * HD
    lane = lax.broadcasted_iota(jnp.int32, (tok, lanes), 1)
    low = lane < HD
    head = lax.broadcasted_iota(jnp.int32, (tok, H), 1)
    for h in range(width // HD):
        at = slice(h * tok, (h + 1) * tok)
        two = slice((h // 2) * lanes, (h // 2 + 1) * lanes)
        q2 = q_ref[:, two].astype(jnp.float32) * SCALE
        g2 = g_ref[:, two].astype(jnp.float32)
        if h % 2:
            q2 = pltpu.roll(q2, HD, 1)
            g2 = pltpu.roll(g2, HD, 1)
        mine = jnp.sum(jnp.where(head == h, cl_ref[...], 0), axis=1, keepdims=True)
        same = jnp.where(mine >= HD, mine - HD, mine)
        first = jnp.where(lane - HD == mine, 1.0, 0.0)
        second = jnp.where(lane == jnp.where(low, mine - HD, same + HD), 1.0, 0.0)
        lhs[0, at, :] = jnp.where(low, q2, first).astype(jnp.bfloat16)
        lhs[1, at, :] = second.astype(jnp.bfloat16)
        grd[at, :] = g2[:, :HD].astype(jnp.bfloat16)


def prepare_rows(queries, out_grad, cluster_of):
    tok, width = queries.shape
    rows = width // HD * tok
    return pl.pallas_call(
        prepare_rows_kernel,
        out_shape=(
            jax.ShapeDtypeStruct((2, rows, 2 * HD), jnp.bfloat16),
            jax.ShapeDtypeStruct((rows, HD), jnp.bfloat16),
        ),
        cost_estimate=pl.CostEstimate(flops=10**7, bytes_accessed=2 * 10**6, transcendentals=0),
    )(queries, out_grad, cluster_of)


def prepare_keys_kernel(*refs):
    kv_refs = refs[:-3]
    rhs, val, key = refs[-3:]
    tok = rhs.shape[2]
    quarter = HD // 2
    ids = lax.broadcasted_iota(jnp.int32, (quarter, tok), 0)
    at = 0
    for kv_ref in kv_refs:
        for j in range(kv_ref.shape[0]):
            kv = kv_ref[j, 0:tok, :]
            turned = kv.astype(jnp.float32).T.astype(jnp.bfloat16)
            rhs[at, 0:HD, :] = turned[:HD]
            val[at, :, :] = turned[HD:]
            key[at * tok : (at + 1) * tok, :] = kv
            cl = kv_ref[j, tok : tok + H, :].astype(jnp.float32).astype(jnp.int32)
            group = jnp.bitwise_and(cl, quarter - 1)
            one = jnp.left_shift(1, 8 * jnp.right_shift(cl, 5))
            packed = jnp.zeros((quarter, tok), jnp.int32)
            for h in range(H):
                packed += jnp.where(group[h : h + 1, :] == ids, one[h : h + 1, :], 0)
            res = []
            for part in range(4):
                count = jnp.bitwise_and(jnp.right_shift(packed, 8 * part), 255)
                live = count > 0
                log = jnp.log(count.astype(jnp.float32))
                hi = jnp.where(live, log, -1e30).astype(jnp.bfloat16)
                rhs[at, HD + part * quarter : HD + (part + 1) * quarter, :] = hi
                res.append(jnp.where(live, log - hi.astype(jnp.float32), 0.0))
            for part in range(2):
                a, b = res[part], res[part + 2]
                both = jnp.where(a == 0.0, b, jnp.where(b == 0.0, a, 0.5 * (a + b)))
                start = 3 * HD + part * quarter
                rhs[at, start : start + quarter, :] = both.astype(jnp.bfloat16)
            at += 1


def prepare_keys(gathered):
    tok = gathered[0].shape[2]
    blocks = sum(g.shape[0] for g in gathered)
    return pl.pallas_call(
        prepare_keys_kernel,
        out_shape=(
            jax.ShapeDtypeStruct((blocks, 4 * HD, tok), jnp.bfloat16),
            jax.ShapeDtypeStruct((blocks, HD, tok), jnp.bfloat16),
            jax.ShapeDtypeStruct((blocks * tok, 2 * HD), jnp.bfloat16),
        ),
        cost_estimate=pl.CostEstimate(
            flops=blocks * 10**6, bytes_accessed=blocks * 10**5, transcendentals=0
        ),
    )(*gathered)


def attend_kernel(lhs, grd, *refs):
    count = (len(refs) - 9) // 3
    groups = [refs[3 * i : 3 * i + 3] for i in range(count)]
    out_ref, sc0, sc1, pg0, pg1, ds0, ds1, acc, tot = refs[3 * count :]
    sc, pg, ds = (sc0, sc1), (pg0, pg1), (ds0, ds1)
    lanes = 2 * HD
    tok = out_ref.shape[0]
    rows = sc0.shape[0]
    per = TILE // lanes
    places = [(g, j) for g, group in enumerate(groups) for j in range(group[0].shape[0] // per)]
    tiles = len(places)
    total = tiles * TILE
    steps = out_ref.shape[1] // HD * tok // rows
    block = rows // tiles
    chunks = [slice(c * lanes, (c + 1) * lanes) for c in range(total // lanes)]

    def gated(x, gate):
        if gate is None:
            return x
        tie = jnp.tile((gate * 0.0).astype(x.dtype), (1, x.shape[1] // gate.shape[1]))
        pieces = []
        for r in range(0, x.shape[0], 2 * lanes):
            pieces += [x[r : r + 16] + tie, x[r + 16 : r + 2 * lanes]]
        return jnp.concatenate(pieces, axis=0)

    def score(step, slot, t, gate=None):
        g, j = places[t]
        at = pl.ds(pl.multiple_of(step * rows, rows), rows)
        span = range(j * per, (j + 1) * per)
        right = jnp.concatenate([groups[g][0][b] for b in span], axis=1)
        left = jnp.concatenate([lhs[0, at, :], lhs[1, at, :]], axis=1)
        cols = slice(t * TILE, (t + 1) * TILE)
        sc[slot][:, cols] = jnp.dot(left, gated(right, gate), preferred_element_type=jnp.float32)
        right = jnp.concatenate([groups[g][1][b] for b in span], axis=1)
        pg[slot][:, cols] = jnp.dot(
            grd[at, :], gated(right, gate), preferred_element_type=jnp.float32
        )

    def soften(slot, t):
        at = slice(t * block, (t + 1) * block)
        top = sc[slot][at, chunks[0]]
        for c in chunks[1:]:
            top = jnp.maximum(top, sc[slot][at, c])
        top = jnp.broadcast_to(jnp.max(top, axis=1, keepdims=True), (block, lanes))
        denom = jnp.zeros((block, lanes), jnp.float32)
        dots = jnp.zeros((block, lanes), jnp.float32)
        for c in chunks:
            w = jnp.exp(sc[slot][at, c] - top)
            sc[slot][at, c] = w
            denom += w
            dots += w * pg[slot][at, c]
        denom = jnp.sum(denom, axis=1, keepdims=True)
        inv = jnp.broadcast_to(SCALE / denom, (block, lanes))
        dot = jnp.broadcast_to(jnp.sum(dots, axis=1, keepdims=True) / denom, (block, lanes))
        for i, c in enumerate(chunks):
            d = (sc[slot][at, c] * inv) * (pg[slot][at, c] - dot)
            ds[slot][i, at, :] = d.astype(jnp.bfloat16)
        return d[0:16, :]

    def collect(slot, t, gate=None):
        g, j = places[t]
        left = jnp.concatenate([ds[slot][t * per + b] for b in range(per)], axis=1)
        right = gated(groups[g][2][j * TILE : (j + 1) * TILE, :], gate)
        add = jnp.dot(left, right, preferred_element_type=jnp.float32)
        acc[...] = add if t == 0 else acc[...] + add

    def finish(step):
        low = lax.broadcasted_iota(jnp.int32, (tok, lanes), 1) < HD
        for j in range(rows // (2 * tok)):
            even = acc[2 * j * tok : (2 * j + 1) * tok, :]
            odd = pltpu.roll(acc[(2 * j + 1) * tok : (2 * j + 2) * tok, :], HD, 1)
            where = pl.multiple_of((step * (rows // (2 * tok)) + j) * lanes, lanes)
            out_ref[:, pl.ds(where, lanes)] = jnp.where(low, even, odd).astype(jnp.bfloat16)

    def stage(step, slot, following):
        gate = None
        for t in range(tiles):
            score(following, 1 - slot, t, gate)
            collect(1 - slot, t, gate)
            gate = soften(slot, t)

        @pl.when(step > 0)
        def _():
            finish(step - 1)

    for t in range(tiles):
        score(0, 0, t)

    def body(i, _):
        stage(2 * i, 0, 2 * i + 1)
        stage(2 * i + 1, 1, jnp.minimum(2 * i + 2, steps - 1))
        return 0

    lax.fori_loop(0, steps // 2, body, 0)
    for t in range(tiles):
        collect(1, t)
    finish(steps - 1)


def attend(left, groups, tok):
    lhs, grd = left
    heads = grd.shape[0] // tok
    total = sum(g[2].shape[0] for g in groups)
    lanes = 2 * HD
    rows = 2 * tok
    operands = [lhs, grd] + [x for g in groups for x in g]
    work = grd.shape[0] * total
    return pl.pallas_call(
        attend_kernel,
        in_specs=[pl.BlockSpec(memory_space=pltpu.VMEM)] * len(operands),
        out_specs=pl.BlockSpec(memory_space=pltpu.VMEM),
        out_shape=jax.ShapeDtypeStruct((tok, heads * HD), jnp.bfloat16),
        scratch_shapes=[pltpu.VMEM((rows, total), jnp.float32)] * 4
        + [pltpu.VMEM((total // lanes, rows, lanes), jnp.bfloat16)] * 2
        + [pltpu.VMEM((rows, lanes), jnp.float32)] * 2,
        compiler_params=pltpu.CompilerParams(vmem_limit_bytes=40 * 1024 * 1024),
        cost_estimate=pl.CostEstimate(
            flops=work * 6 * HD, bytes_accessed=10**7, transcendentals=work
        ),
    )(*operands)


def bench(q, g, c, *parts):
    groups = [prepare_keys(parts[:1]), prepare_keys(parts[1:4]), prepare_keys(parts[4:])]
    return attend(prepare_rows(q, g, c), groups, q.shape[0])


def xor_permute(x, axis, mask):
    n = lax.axis_size(axis)
    return lax.ppermute(x, axis, [(i, i ^ mask) for i in range(n)])


def dense(tokens_in, queries, key_value, out_grad, cluster_of, slot_of):
    n = lax.axis_size("seq")
    tok, width = queries.shape
    me = lax.axis_index("pair")
    low = 1
    while low * low < n:
        low *= 2
    high = n // low
    own = jnp.concatenate([key_value, cluster_of.T.astype(jnp.bfloat16)], axis=0)[None]
    column = jnp.concatenate([own] + [xor_permute(own, "seq", low * k) for k in range(1, high)])
    near = [xor_permute(column, "seq", k) for k in range(1, low)]
    left = prepare_rows(queries, out_grad, cluster_of)
    groups = [
        prepare_keys([column]),
        prepare_keys(near),
        prepare_keys([xor_permute(p, "pair", 1) for p in [column] + near]),
    ]

    depth = tokens_in.shape[1]
    x4 = tokens_in.reshape(tok, n, 2, depth // (2 * n))
    x_mine = lax.dynamic_index_in_dim(x4, me, 2, keepdims=False).reshape(tok, depth // 2)
    x_other = lax.dynamic_index_in_dim(x4, 1 - me, 2, keepdims=False).reshape(tok, depth // 2)
    x_got = xor_permute(x_other, "pair", 1)

    mine = attend(left, groups, tok)
    other = xor_permute(mine, "pair", 1)
    contract = (((0,), (0,)), ((), ()))
    block = lax.dot_general(
        x_mine, mine, contract, preferred_element_type=jnp.float32
    ) + lax.dot_general(x_got, other, contract, preferred_element_type=jnp.float32)
    block = block.astype(jnp.bfloat16).reshape(n, depth // (2 * n), width)
    got = lax.all_to_all(block, "seq", 0, 0, tiled=True)
    return jnp.sum(got.astype(jnp.float32), axis=0)


def cluster_grad(query_part, key_part, live_keys):
    query_rows = query_part[:, :HD]
    grad_rows = query_part[:, HD:]
    key_rows = key_part[:, :HD]
    value_rows = key_part[:, HD:]
    scores = jnp.dot(query_rows, key_rows.T, preferred_element_type=jnp.float32) * SCALE
    scores = jnp.where(live_keys[None, :] > 0, scores, jnp.float32(-1e30))
    row_max = jnp.max(scores, axis=1, keepdims=True)
    weights = jnp.exp(scores - row_max)
    probs = weights / jnp.sum(weights, axis=1, keepdims=True)
    prob_grad = jnp.dot(grad_rows, value_rows.T, preferred_element_type=jnp.float32)
    row_dot = jnp.sum(probs * prob_grad, axis=1, keepdims=True)
    score_grad = (probs * (prob_grad - row_dot) * SCALE).astype(jnp.bfloat16)
    return jnp.dot(score_grad, key_rows, preferred_element_type=jnp.float32).astype(jnp.bfloat16)


def routed(tokens_in, queries, key_value, out_grad, cluster_of, slot_of):
    groups = lax.axis_size("seq")
    tok_count = queries.shape[0]
    row_count = tok_count * H
    bound_rows = 2 * row_count // groups
    slot_count = CL_DEV * HALF
    owners = (cluster_of // CL_DEV).reshape(row_count)
    local_slot = (cluster_of % CL_DEV * HALF + slot_of % HALF).reshape(row_count)
    picked = (owners[:, None] == jnp.arange(groups, dtype=jnp.int32)[None, :]).astype(jnp.int32)
    ranked = jnp.sum(jnp.cumsum(picked, axis=0) * picked, axis=1) - 1
    cell_index = owners * bound_rows + ranked
    paired_rows = jnp.concatenate(
        [queries.reshape(row_count, HD), out_grad.reshape(row_count, HD)], axis=1
    )
    packed = jnp.concatenate([paired_rows, jnp.repeat(key_value, H, axis=0)], axis=1)
    outgoing = jnp.zeros((groups * bound_rows, 4 * HD), jnp.bfloat16).at[cell_index].set(packed)
    labels = jnp.full((groups * bound_rows,), -1, jnp.int32).at[cell_index].set(local_slot)
    incoming = lax.all_to_all(
        outgoing.reshape(groups, bound_rows, 4 * HD), "seq", 0, 0, tiled=True
    )
    labels_in = lax.all_to_all(labels.reshape(groups, bound_rows), "seq", 0, 0, tiled=True)
    target = labels_in.reshape(groups * bound_rows)
    target_safe = jnp.where(target >= 0, target, slot_count)
    arranged = (
        jnp.zeros((slot_count, 4 * HD), jnp.bfloat16)
        .at[target_safe]
        .set(incoming.reshape(groups * bound_rows, 4 * HD), mode="drop")
    )
    live_slot = (
        jnp.zeros((slot_count,), jnp.bfloat16)
        .at[target_safe]
        .set(jnp.ones((groups * bound_rows,), jnp.bfloat16), mode="drop")
    )
    arranged = arranged.reshape(CL_DEV, HALF, 4 * HD)
    keys_all = lax.all_gather(arranged[:, :, 2 * HD :], "pair", axis=1, tiled=True)
    live_all = lax.all_gather(live_slot.reshape(CL_DEV, HALF), "pair", axis=1, tiled=True)
    cluster_grads = lax.map(
        lambda ops: cluster_grad(*ops), (arranged[:, :, : 2 * HD], keys_all, live_all)
    )
    slot_grads = cluster_grads.reshape(slot_count, HD)
    going_back = jnp.where(
        target[:, None] >= 0,
        slot_grads[jnp.minimum(target_safe, slot_count - 1)],
        jnp.zeros((), jnp.bfloat16),
    )
    returned = lax.all_to_all(
        going_back.reshape(groups, bound_rows // 2, 2 * HD), "seq", 0, 0, tiled=True
    )
    query_grad = returned.reshape(groups * bound_rows, HD)[cell_index].reshape(tok_count, H * HD)
    partial_rows = lax.psum_scatter(
        lax.dot_general(
            tokens_in, query_grad, (((0,), (0,)), ((), ())), preferred_element_type=jnp.float32
        ),
        "seq",
        scatter_dimension=0,
        tiled=True,
    )
    return lax.psum_scatter(partial_rows, "pair", scatter_dimension=0, tiled=True)


def solution(mesh):
    n = mesh.shape["seq"]
    small = n * CL_DEV == 2 * HD and n & (n - 1) == 0
    spec = P(("seq", "pair"), None)
    return jax.shard_map(
        dense if small else routed,
        mesh=mesh,
        in_specs=(spec,) * 6,
        out_specs=spec,
        check_vma=False,
    )
```

```python
import jax
import jax.numpy as jnp
from jax import lax
from jax.experimental import pallas as pl
from jax.experimental.pallas import tpu as pltpu
from jax.sharding import PartitionSpec as P

H = 16
HD = 64
HALF = 512
CL_DEV = 8
SCALE = HD ** (-0.5)
LOG2E = 1.4426950408889634
TILE = 512


def prepare_rows_kernel(q_ref, g_ref, cl_ref, lhs, grd):
    tok, width = q_ref.shape
    lanes = 2 * HD
    lane = lax.broadcasted_iota(jnp.int32, (tok, lanes), 1)
    low = lane < HD
    head = lax.broadcasted_iota(jnp.int32, (tok, H), 1)
    for h in range(width // HD):
        at = slice(h * tok, (h + 1) * tok)
        two = slice((h // 2) * lanes, (h // 2 + 1) * lanes)
        q2 = q_ref[:, two].astype(jnp.float32) * SCALE
        g2 = g_ref[:, two].astype(jnp.float32)
        if h % 2:
            q2 = pltpu.roll(q2, HD, 1)
            g2 = pltpu.roll(g2, HD, 1)
        mine = jnp.sum(jnp.where(head == h, cl_ref[...], 0), axis=1, keepdims=True)
        same = jnp.where(mine >= HD, mine - HD, mine)
        first = jnp.where(lane - HD == mine, 1.0, 0.0)
        second = jnp.where(lane == jnp.where(low, mine - HD, same + HD), 1.0, 0.0)
        lhs[0, at, :] = jnp.where(low, q2, first).astype(jnp.bfloat16)
        lhs[1, at, :] = second.astype(jnp.bfloat16)
        grd[at, :] = g2[:, :HD].astype(jnp.bfloat16)


def prepare_rows(queries, out_grad, cluster_of):
    tok, width = queries.shape
    rows = width // HD * tok
    return pl.pallas_call(
        prepare_rows_kernel,
        out_shape=(
            jax.ShapeDtypeStruct((2, rows, 2 * HD), jnp.bfloat16),
            jax.ShapeDtypeStruct((rows, HD), jnp.bfloat16),
        ),
        compiler_params=pltpu.CompilerParams(vmem_limit_bytes=8 * 1024 * 1024),
        cost_estimate=pl.CostEstimate(flops=10**7, bytes_accessed=2 * 10**6, transcendentals=0),
    )(queries, out_grad, cluster_of)


def prepare_keys_kernel(*refs):
    kv_refs = refs[:-3]
    rhs, val, key = refs[-3:]
    tok = rhs.shape[2]
    quarter = HD // 2
    ids = lax.broadcasted_iota(jnp.int32, (quarter, tok), 0)
    at = 0
    for kv_ref in kv_refs:
        for j in range(kv_ref.shape[0]):
            kv = kv_ref[j, 0:tok, :]
            turned = kv.astype(jnp.float32).T.astype(jnp.bfloat16)
            rhs[at, 0:HD, :] = turned[:HD]
            val[at, :, :] = turned[HD:]
            key[at * tok : (at + 1) * tok, :] = kv
            cl = kv_ref[j, tok : tok + H, :].astype(jnp.float32).astype(jnp.int32)
            group = jnp.bitwise_and(cl, quarter - 1)
            one = jnp.left_shift(1, 8 * jnp.right_shift(cl, 5))
            packed = jnp.zeros((quarter, tok), jnp.int32)
            for h in range(H):
                packed += jnp.where(group[h : h + 1, :] == ids, one[h : h + 1, :], 0)
            res = []
            for part in range(4):
                count = jnp.bitwise_and(jnp.right_shift(packed, 8 * part), 255)
                live = count > 0
                log = jnp.log(count.astype(jnp.float32))
                hi = jnp.where(live, log, -1e30).astype(jnp.bfloat16)
                rhs[at, HD + part * quarter : HD + (part + 1) * quarter, :] = hi
                res.append(jnp.where(live, log - hi.astype(jnp.float32), 0.0))
            for part in range(2):
                a, b = res[part], res[part + 2]
                both = jnp.where(a == 0.0, b, jnp.where(b == 0.0, a, 0.5 * (a + b)))
                start = 3 * HD + part * quarter
                rhs[at, start : start + quarter, :] = both.astype(jnp.bfloat16)
            at += 1


def prepare_keys(gathered):
    tok = gathered[0].shape[2]
    blocks = sum(g.shape[0] for g in gathered)
    return pl.pallas_call(
        prepare_keys_kernel,
        out_shape=(
            jax.ShapeDtypeStruct((blocks, 4 * HD, tok), jnp.bfloat16),
            jax.ShapeDtypeStruct((blocks, HD, tok), jnp.bfloat16),
            jax.ShapeDtypeStruct((blocks * tok, 2 * HD), jnp.bfloat16),
        ),
        compiler_params=pltpu.CompilerParams(vmem_limit_bytes=8 * 1024 * 1024),
        cost_estimate=pl.CostEstimate(
            flops=blocks * 10**6, bytes_accessed=blocks * 10**5, transcendentals=0
        ),
    )(*gathered)


def attend_kernel(lhs, grd, *refs):
    count = (len(refs) - 9) // 3
    groups = [refs[3 * i : 3 * i + 3] for i in range(count)]
    out_ref, sc0, sc1, pg0, pg1, ds0, ds1, acc, tot = refs[3 * count :]
    sc, pg, ds = (sc0, sc1), (pg0, pg1), (ds0, ds1)
    lanes = 2 * HD
    tok = out_ref.shape[0]
    rows = sc0.shape[0]
    per = TILE // lanes
    places = [(g, j) for g, group in enumerate(groups) for j in range(group[0].shape[0] // per)]
    tiles = len(places)
    total = tiles * TILE
    steps = out_ref.shape[1] // HD * tok // rows
    block = rows // tiles
    chunks = [slice(c * lanes, (c + 1) * lanes) for c in range(total // lanes)]

    def gated(x, gate):
        if gate is None:
            return x
        tie = jnp.tile((gate * 0.0).astype(x.dtype), (1, x.shape[1] // gate.shape[1]))
        pieces = []
        for r in range(0, x.shape[0], 2 * lanes):
            pieces += [x[r : r + 16] + tie, x[r + 16 : r + 2 * lanes]]
        return jnp.concatenate(pieces, axis=0)

    def score(step, slot, t, gate=None):
        g, j = places[t]
        at = pl.ds(pl.multiple_of(step * rows, rows), rows)
        span = range(j * per, (j + 1) * per)
        right = jnp.concatenate([groups[g][0][b] for b in span], axis=1)
        left = jnp.concatenate([lhs[0, at, :], lhs[1, at, :]], axis=1)
        cols = slice(t * TILE, (t + 1) * TILE)
        sc[slot][:, cols] = jnp.dot(left, gated(right, gate), preferred_element_type=jnp.float32)
        right = jnp.concatenate([groups[g][1][b] for b in span], axis=1)
        pg[slot][:, cols] = jnp.dot(
            grd[at, :], gated(right, gate), preferred_element_type=jnp.float32
        )

    def soften(slot, t):
        at = slice(t * block, (t + 1) * block)
        top = sc[slot][at, chunks[0]]
        for c in chunks[1:]:
            top = jnp.maximum(top, sc[slot][at, c])
        top = jnp.broadcast_to(jnp.max(top, axis=1, keepdims=True), (block, lanes))
        denom = jnp.zeros((block, lanes), jnp.float32)
        dots = jnp.zeros((block, lanes), jnp.float32)
        for c in chunks:
            w = jnp.exp(sc[slot][at, c] - top)
            sc[slot][at, c] = w
            denom += w
            dots += w * pg[slot][at, c]
        denom = jnp.sum(denom, axis=1, keepdims=True)
        inv = jnp.broadcast_to(SCALE / denom, (block, lanes))
        dot = jnp.broadcast_to(jnp.sum(dots, axis=1, keepdims=True) / denom, (block, lanes))
        for i, c in enumerate(chunks):
            d = (sc[slot][at, c] * inv) * (pg[slot][at, c] - dot)
            ds[slot][i, at, :] = d.astype(jnp.bfloat16)
        return d[0:16, :]

    def collect(slot, t, gate=None):
        g, j = places[t]
        left = jnp.concatenate([ds[slot][t * per + b] for b in range(per)], axis=1)
        right = gated(groups[g][2][j * TILE : (j + 1) * TILE, :], gate)
        add = jnp.dot(left, right, preferred_element_type=jnp.float32)
        acc[...] = add if t == 0 else acc[...] + add

    def finish(step):
        low = lax.broadcasted_iota(jnp.int32, (tok, lanes), 1) < HD
        for j in range(rows // (2 * tok)):
            even = acc[2 * j * tok : (2 * j + 1) * tok, :]
            odd = pltpu.roll(acc[(2 * j + 1) * tok : (2 * j + 2) * tok, :], HD, 1)
            where = pl.multiple_of((step * (rows // (2 * tok)) + j) * lanes, lanes)
            out_ref[:, pl.ds(where, lanes)] = jnp.where(low, even, odd).astype(jnp.bfloat16)

    def stage(step, slot, following):
        gate = None
        for t in range(tiles):
            score(following, 1 - slot, t, gate)
            collect(1 - slot, t, gate)
            gate = soften(slot, t)

        @pl.when(step > 0)
        def _():
            finish(step - 1)

    for t in range(tiles):
        score(0, 0, t)

    def body(i, _):
        stage(2 * i, 0, 2 * i + 1)
        stage(2 * i + 1, 1, jnp.minimum(2 * i + 2, steps - 1))
        return 0

    lax.fori_loop(0, steps // 2, body, 0)
    for t in range(tiles):
        collect(1, t)
    finish(steps - 1)


def attend(left, groups, tok):
    lhs, grd = left
    heads = grd.shape[0] // tok
    total = sum(g[2].shape[0] for g in groups)
    lanes = 2 * HD
    rows = 2 * tok
    operands = [lhs, grd] + [x for g in groups for x in g]
    work = grd.shape[0] * total
    return pl.pallas_call(
        attend_kernel,
        in_specs=[pl.BlockSpec(memory_space=pltpu.VMEM)] * len(operands),
        out_specs=pl.BlockSpec(memory_space=pltpu.VMEM),
        out_shape=jax.ShapeDtypeStruct((tok, heads * HD), jnp.bfloat16),
        scratch_shapes=[pltpu.VMEM((rows, total), jnp.float32)] * 4
        + [pltpu.VMEM((total // lanes, rows, lanes), jnp.bfloat16)] * 2
        + [pltpu.VMEM((rows, lanes), jnp.float32)] * 2,
        compiler_params=pltpu.CompilerParams(vmem_limit_bytes=40 * 1024 * 1024),
        cost_estimate=pl.CostEstimate(
            flops=work * 6 * HD, bytes_accessed=10**7, transcendentals=work
        ),
    )(*operands)


def bench(q, g, c, *parts):
    groups = [prepare_keys(parts[:1]), prepare_keys(parts[1:4]), prepare_keys(parts[4:])]
    return attend(prepare_rows(q, g, c), groups, q.shape[0])


def xor_permute(x, axis, mask):
    n = lax.axis_size(axis)
    return lax.ppermute(x, axis, [(i, i ^ mask) for i in range(n)])


def dense(tokens_in, queries, key_value, out_grad, cluster_of, slot_of):
    n = lax.axis_size("seq")
    tok, width = queries.shape
    me = lax.axis_index("pair")
    low = 1
    while low * low < n:
        low *= 2
    high = n // low
    own = jnp.concatenate([key_value, cluster_of.T.astype(jnp.bfloat16)], axis=0)[None]
    column = jnp.concatenate([own] + [xor_permute(own, "seq", low * k) for k in range(1, high)])
    near = [xor_permute(column, "seq", k) for k in range(1, low)]
    left = prepare_rows(queries, out_grad, cluster_of)
    groups = [
        prepare_keys([column]),
        prepare_keys(near),
        prepare_keys([xor_permute(p, "pair", 1) for p in [column] + near]),
    ]

    depth = tokens_in.shape[1]
    x4 = tokens_in.reshape(tok, n, 2, depth // (2 * n))
    x_mine = lax.dynamic_index_in_dim(x4, me, 2, keepdims=False).reshape(tok, depth // 2)
    x_other = lax.dynamic_index_in_dim(x4, 1 - me, 2, keepdims=False).reshape(tok, depth // 2)
    x_got = xor_permute(x_other, "pair", 1)

    mine = attend(left, groups, tok)
    other = xor_permute(mine, "pair", 1)
    contract = (((0,), (0,)), ((), ()))
    block = lax.dot_general(
        x_mine, mine, contract, preferred_element_type=jnp.float32
    ) + lax.dot_general(x_got, other, contract, preferred_element_type=jnp.float32)
    block = block.astype(jnp.bfloat16).reshape(n, depth // (2 * n), width)
    got = lax.all_to_all(block, "seq", 0, 0, tiled=True)
    return jnp.sum(got.astype(jnp.float32), axis=0)


def cluster_grad(query_part, key_part, live_keys):
    query_rows = query_part[:, :HD]
    grad_rows = query_part[:, HD:]
    key_rows = key_part[:, :HD]
    value_rows = key_part[:, HD:]
    scores = jnp.dot(query_rows, key_rows.T, preferred_element_type=jnp.float32) * SCALE
    scores = jnp.where(live_keys[None, :] > 0, scores, jnp.float32(-1e30))
    row_max = jnp.max(scores, axis=1, keepdims=True)
    weights = jnp.exp(scores - row_max)
    probs = weights / jnp.sum(weights, axis=1, keepdims=True)
    prob_grad = jnp.dot(grad_rows, value_rows.T, preferred_element_type=jnp.float32)
    row_dot = jnp.sum(probs * prob_grad, axis=1, keepdims=True)
    score_grad = (probs * (prob_grad - row_dot) * SCALE).astype(jnp.bfloat16)
    return jnp.dot(score_grad, key_rows, preferred_element_type=jnp.float32).astype(jnp.bfloat16)


def routed(tokens_in, queries, key_value, out_grad, cluster_of, slot_of):
    groups = lax.axis_size("seq")
    tok_count = queries.shape[0]
    row_count = tok_count * H
    bound_rows = 2 * row_count // groups
    slot_count = CL_DEV * HALF
    owners = (cluster_of // CL_DEV).reshape(row_count)
    local_slot = (cluster_of % CL_DEV * HALF + slot_of % HALF).reshape(row_count)
    picked = (owners[:, None] == jnp.arange(groups, dtype=jnp.int32)[None, :]).astype(jnp.int32)
    ranked = jnp.sum(jnp.cumsum(picked, axis=0) * picked, axis=1) - 1
    cell_index = owners * bound_rows + ranked
    paired_rows = jnp.concatenate(
        [queries.reshape(row_count, HD), out_grad.reshape(row_count, HD)], axis=1
    )
    packed = jnp.concatenate([paired_rows, jnp.repeat(key_value, H, axis=0)], axis=1)
    outgoing = jnp.zeros((groups * bound_rows, 4 * HD), jnp.bfloat16).at[cell_index].set(packed)
    labels = jnp.full((groups * bound_rows,), -1, jnp.int32).at[cell_index].set(local_slot)
    incoming = lax.all_to_all(
        outgoing.reshape(groups, bound_rows, 4 * HD), "seq", 0, 0, tiled=True
    )
    labels_in = lax.all_to_all(labels.reshape(groups, bound_rows), "seq", 0, 0, tiled=True)
    target = labels_in.reshape(groups * bound_rows)
    target_safe = jnp.where(target >= 0, target, slot_count)
    arranged = (
        jnp.zeros((slot_count, 4 * HD), jnp.bfloat16)
        .at[target_safe]
        .set(incoming.reshape(groups * bound_rows, 4 * HD), mode="drop")
    )
    live_slot = (
        jnp.zeros((slot_count,), jnp.bfloat16)
        .at[target_safe]
        .set(jnp.ones((groups * bound_rows,), jnp.bfloat16), mode="drop")
    )
    arranged = arranged.reshape(CL_DEV, HALF, 4 * HD)
    keys_all = lax.all_gather(arranged[:, :, 2 * HD :], "pair", axis=1, tiled=True)
    live_all = lax.all_gather(live_slot.reshape(CL_DEV, HALF), "pair", axis=1, tiled=True)
    cluster_grads = lax.map(
        lambda ops: cluster_grad(*ops), (arranged[:, :, : 2 * HD], keys_all, live_all)
    )
    slot_grads = cluster_grads.reshape(slot_count, HD)
    going_back = jnp.where(
        target[:, None] >= 0,
        slot_grads[jnp.minimum(target_safe, slot_count - 1)],
        jnp.zeros((), jnp.bfloat16),
    )
    returned = lax.all_to_all(
        going_back.reshape(groups, bound_rows // 2, 2 * HD), "seq", 0, 0, tiled=True
    )
    query_grad = returned.reshape(groups * bound_rows, HD)[cell_index].reshape(tok_count, H * HD)
    partial_rows = lax.psum_scatter(
        lax.dot_general(
            tokens_in, query_grad, (((0,), (0,)), ((), ())), preferred_element_type=jnp.float32
        ),
        "seq",
        scatter_dimension=0,
        tiled=True,
    )
    return lax.psum_scatter(partial_rows, "pair", scatter_dimension=0, tiled=True)


def solution(mesh):
    n = mesh.shape["seq"]
    small = n * CL_DEV == 2 * HD and n & (n - 1) == 0
    spec = P(("seq", "pair"), None)
    return jax.shard_map(
        dense if small else routed,
        mesh=mesh,
        in_specs=(spec,) * 6,
        out_specs=spec,
        check_vma=False,
    )
```

```python
import jax
import jax.numpy as jnp
from jax import lax
from jax.experimental import pallas as pl
from jax.experimental.pallas import tpu as pltpu
from jax.sharding import PartitionSpec as P

H = 16
HD = 64
HALF = 512
CL_DEV = 8
SCALE = HD ** (-0.5)
LOG2E = 1.4426950408889634
TILE = 512
LAG = 2
GAP = 4


def prepare_rows_kernel(q_ref, g_ref, cl_ref, lhs, grd):
    tok, width = q_ref.shape
    lanes = 2 * HD
    lane = lax.broadcasted_iota(jnp.int32, (tok, lanes), 1)
    low = lane < HD
    head = lax.broadcasted_iota(jnp.int32, (tok, H), 1)
    for h in range(width // HD):
        at = slice(h * tok, (h + 1) * tok)
        two = slice((h // 2) * lanes, (h // 2 + 1) * lanes)
        q2 = q_ref[:, two].astype(jnp.float32) * SCALE
        g2 = g_ref[:, two].astype(jnp.float32)
        if h % 2:
            q2 = pltpu.roll(q2, HD, 1)
            g2 = pltpu.roll(g2, HD, 1)
        mine = jnp.sum(jnp.where(head == h, cl_ref[...], 0), axis=1, keepdims=True)
        same = jnp.where(mine >= HD, mine - HD, mine)
        first = jnp.where(lane - HD == mine, 1.0, 0.0)
        second = jnp.where(lane == jnp.where(low, mine - HD, same + HD), 1.0, 0.0)
        lhs[0, at, :] = jnp.where(low, q2, first).astype(jnp.bfloat16)
        lhs[1, at, :] = second.astype(jnp.bfloat16)
        grd[at, :] = g2[:, :HD].astype(jnp.bfloat16)


def prepare_rows(queries, out_grad, cluster_of):
    tok, width = queries.shape
    rows = width // HD * tok
    return pl.pallas_call(
        prepare_rows_kernel,
        out_shape=(
            jax.ShapeDtypeStruct((2, rows, 2 * HD), jnp.bfloat16),
            jax.ShapeDtypeStruct((rows, HD), jnp.bfloat16),
        ),
        compiler_params=pltpu.CompilerParams(vmem_limit_bytes=8 * 1024 * 1024),
        cost_estimate=pl.CostEstimate(flops=10**7, bytes_accessed=2 * 10**6, transcendentals=0),
    )(queries, out_grad, cluster_of)


def prepare_keys_kernel(*refs):
    kv_refs = refs[:-3]
    rhs, val, key = refs[-3:]
    tok = rhs.shape[2]
    quarter = HD // 2
    ids = lax.broadcasted_iota(jnp.int32, (quarter, tok), 0)
    at = 0
    for kv_ref in kv_refs:
        for j in range(kv_ref.shape[0]):
            kv = kv_ref[j, 0:tok, :]
            turned = kv.astype(jnp.float32).T.astype(jnp.bfloat16)
            rhs[at, 0:HD, :] = turned[:HD]
            val[at, :, :] = turned[HD:]
            key[at * tok : (at + 1) * tok, :] = kv
            cl = kv_ref[j, tok : tok + H, :].astype(jnp.float32).astype(jnp.int32)
            group = jnp.bitwise_and(cl, quarter - 1)
            one = jnp.left_shift(1, 8 * jnp.right_shift(cl, 5))
            packed = jnp.zeros((quarter, tok), jnp.int32)
            for h in range(H):
                packed += jnp.where(group[h : h + 1, :] == ids, one[h : h + 1, :], 0)
            res = []
            for part in range(4):
                count = jnp.bitwise_and(jnp.right_shift(packed, 8 * part), 255)
                live = count > 0
                log = jnp.log(count.astype(jnp.float32))
                hi = jnp.where(live, log, -1e30).astype(jnp.bfloat16)
                rhs[at, HD + part * quarter : HD + (part + 1) * quarter, :] = hi
                res.append(jnp.where(live, log - hi.astype(jnp.float32), 0.0))
            for part in range(2):
                a, b = res[part], res[part + 2]
                both = jnp.where(a == 0.0, b, jnp.where(b == 0.0, a, 0.5 * (a + b)))
                start = 3 * HD + part * quarter
                rhs[at, start : start + quarter, :] = both.astype(jnp.bfloat16)
            at += 1


def prepare_keys(gathered):
    tok = gathered[0].shape[2]
    blocks = sum(g.shape[0] for g in gathered)
    return pl.pallas_call(
        prepare_keys_kernel,
        out_shape=(
            jax.ShapeDtypeStruct((blocks, 4 * HD, tok), jnp.bfloat16),
            jax.ShapeDtypeStruct((blocks, HD, tok), jnp.bfloat16),
            jax.ShapeDtypeStruct((blocks * tok, 2 * HD), jnp.bfloat16),
        ),
        compiler_params=pltpu.CompilerParams(vmem_limit_bytes=8 * 1024 * 1024),
        cost_estimate=pl.CostEstimate(
            flops=blocks * 10**6, bytes_accessed=blocks * 10**5, transcendentals=0
        ),
    )(*gathered)


def attend_kernel(lhs, grd, *refs):
    count = (len(refs) - 9) // 3
    groups = [refs[3 * i : 3 * i + 3] for i in range(count)]
    out_ref, sc0, sc1, pg0, pg1, ds0, ds1, acc, tot = refs[3 * count :]
    sc, pg, ds = (sc0, sc1), (pg0, pg1), (ds0, ds1)
    lanes = 2 * HD
    tok = out_ref.shape[0]
    rows = sc0.shape[0]
    per = TILE // lanes
    places = [(g, j) for g, group in enumerate(groups) for j in range(group[0].shape[0] // per)]
    tiles = len(places)
    total = tiles * TILE
    steps = out_ref.shape[1] // HD * tok // rows
    block = rows // tiles
    chunks = [slice(c * lanes, (c + 1) * lanes) for c in range(total // lanes)]

    def gated(x, gate):
        if gate is None:
            return x
        tie = jnp.tile((gate * 0.0).astype(x.dtype), (1, x.shape[1] // gate.shape[1]))
        pieces = []
        for r in range(0, x.shape[0], 2 * lanes):
            pieces += [x[r : r + 16] + tie, x[r + 16 : r + 2 * lanes]]
        return jnp.concatenate(pieces, axis=0)

    def score(step, slot, t, gate=None):
        g, j = places[t]
        at = pl.ds(pl.multiple_of(step * rows, rows), rows)
        span = range(j * per, (j + 1) * per)
        right = jnp.concatenate([groups[g][0][b] for b in span], axis=1)
        left = jnp.concatenate([lhs[0, at, :], lhs[1, at, :]], axis=1)
        cols = slice(t * TILE, (t + 1) * TILE)
        sc[slot][:, cols] = jnp.dot(left, gated(right, gate), preferred_element_type=jnp.float32)
        right = jnp.concatenate([groups[g][1][b] for b in span], axis=1)
        pg[slot][:, cols] = jnp.dot(
            grd[at, :], gated(right, gate), preferred_element_type=jnp.float32
        )

    def soften(slot, t):
        at = slice(t * block, (t + 1) * block)
        top = sc[slot][at, chunks[0]]
        for c in chunks[1:]:
            top = jnp.maximum(top, sc[slot][at, c])
        top = jnp.broadcast_to(jnp.max(top, axis=1, keepdims=True), (block, lanes))
        denom = jnp.zeros((block, lanes), jnp.float32)
        dots = jnp.zeros((block, lanes), jnp.float32)
        for c in chunks:
            w = jnp.exp(sc[slot][at, c] - top)
            sc[slot][at, c] = w
            denom += w
            dots += w * pg[slot][at, c]
        denom = jnp.sum(denom, axis=1, keepdims=True)
        inv = jnp.broadcast_to(SCALE / denom, (block, lanes))
        dot = jnp.broadcast_to(jnp.sum(dots, axis=1, keepdims=True) / denom, (block, lanes))
        gate = None
        for i, c in enumerate(chunks):
            d = (sc[slot][at, c] * inv) * (pg[slot][at, c] - dot)
            ds[slot][i, at, :] = d.astype(jnp.bfloat16)
            if i % GAP == GAP - 1:
                gate = d[0:16, :] if gate is None else gate + d[0:16, :]
        return gate

    def collect(slot, t, gate=None):
        g, j = places[t]
        left = jnp.concatenate([ds[slot][t * per + b] for b in range(per)], axis=1)
        right = gated(groups[g][2][j * TILE : (j + 1) * TILE, :], gate)
        add = jnp.dot(left, right, preferred_element_type=jnp.float32)
        acc[...] = add if t == 0 else acc[...] + add

    def finish(step):
        low = lax.broadcasted_iota(jnp.int32, (tok, lanes), 1) < HD
        for j in range(rows // (2 * tok)):
            even = acc[2 * j * tok : (2 * j + 1) * tok, :]
            odd = pltpu.roll(acc[(2 * j + 1) * tok : (2 * j + 2) * tok, :], HD, 1)
            where = pl.multiple_of((step * (rows // (2 * tok)) + j) * lanes, lanes)
            out_ref[:, pl.ds(where, lanes)] = jnp.where(low, even, odd).astype(jnp.bfloat16)

    def stage(step, slot, following):
        gates = [None] * LAG
        for t in range(tiles):
            score(following, 1 - slot, t, gates[t])
            collect(1 - slot, t, gates[t])
            gates.append(soften(slot, t))

        @pl.when(step > 0)
        def _():
            finish(step - 1)

    for t in range(tiles):
        score(0, 0, t)

    def body(i, _):
        stage(2 * i, 0, 2 * i + 1)
        stage(2 * i + 1, 1, jnp.minimum(2 * i + 2, steps - 1))
        return 0

    lax.fori_loop(0, steps // 2, body, 0)
    for t in range(tiles):
        collect(1, t)
    finish(steps - 1)


def attend(left, groups, tok):
    lhs, grd = left
    heads = grd.shape[0] // tok
    total = sum(g[2].shape[0] for g in groups)
    lanes = 2 * HD
    rows = 2 * tok
    operands = [lhs, grd] + [x for g in groups for x in g]
    work = grd.shape[0] * total
    return pl.pallas_call(
        attend_kernel,
        in_specs=[pl.BlockSpec(memory_space=pltpu.VMEM)] * len(operands),
        out_specs=pl.BlockSpec(memory_space=pltpu.VMEM),
        out_shape=jax.ShapeDtypeStruct((tok, heads * HD), jnp.bfloat16),
        scratch_shapes=[pltpu.VMEM((rows, total), jnp.float32)] * 4
        + [pltpu.VMEM((total // lanes, rows, lanes), jnp.bfloat16)] * 2
        + [pltpu.VMEM((rows, lanes), jnp.float32)] * 2,
        compiler_params=pltpu.CompilerParams(vmem_limit_bytes=40 * 1024 * 1024),
        cost_estimate=pl.CostEstimate(
            flops=work * 6 * HD, bytes_accessed=10**7, transcendentals=work
        ),
    )(*operands)


def bench(q, g, c, *parts):
    groups = [prepare_keys(parts[:1]), prepare_keys(parts[1:4]), prepare_keys(parts[4:])]
    return attend(prepare_rows(q, g, c), groups, q.shape[0])


def xor_permute(x, axis, mask):
    n = lax.axis_size(axis)
    return lax.ppermute(x, axis, [(i, i ^ mask) for i in range(n)])


def dense(tokens_in, queries, key_value, out_grad, cluster_of, slot_of):
    n = lax.axis_size("seq")
    tok, width = queries.shape
    depth = tokens_in.shape[1]
    me = lax.axis_index("pair")
    low = 1
    while low * low < n:
        low *= 2
    high = n // low
    part, layer = lax.axis_index("seq") % low, lax.axis_index("seq") // low
    piece = depth // (2 * n)
    tie = lax.optimization_barrier

    own = jnp.concatenate([key_value, cluster_of.T.astype(jnp.bfloat16)], axis=0)[None]
    above = [xor_permute(own, "seq", low * k) for k in range(1, high)]
    left = prepare_rows(queries, out_grad, cluster_of)
    x5 = tokens_in.reshape(tok, high, low, 2, piece).transpose(2, 3, 0, 1, 4)
    x5 = x5.reshape(low, 2, tok, high * piece)
    above[-1], left, x5 = tie((above[-1], left, x5))
    column = jnp.concatenate([own] + above)
    near = [xor_permute(column, "seq", k) for k in range(1, low)]
    first = prepare_keys([column])
    near[-1], first = tie((near[-1], first))
    far = [xor_permute(p, "pair", 1) for p in [column] + near]
    second = prepare_keys(near)
    far[-1], second = tie((far[-1], second))
    groups = [first, second, prepare_keys(far)]

    x_part = [lax.dynamic_index_in_dim(x5, part ^ k, 0, keepdims=False) for k in range(low)]
    x_part = [x_part[0]] + [xor_permute(x_part[k], "seq", k) for k in range(1, low)]
    x_part = jnp.stack(x_part)
    x_mine = lax.dynamic_index_in_dim(x_part, me, 1, keepdims=False)
    x_pair = xor_permute(lax.dynamic_index_in_dim(x_part, 1 - me, 1, keepdims=False), "pair", 1)

    mine = attend(left, groups, tok)

    def product(x, grad):
        return lax.dot_general(
            x, grad, (((0,), (0,)), ((), ())), preferred_element_type=jnp.float32
        )

    grads = [mine] + [xor_permute(mine, "seq", k) for k in range(1, low)]
    block = sum(product(x_mine[k], grads[k]) for k in range(low))
    grads = [xor_permute(g, "pair", 1) for g in grads]
    block = block + sum(product(x_pair[k], grads[k]) for k in range(low))
    block = block.reshape(high, piece, width)
    total = lax.dynamic_index_in_dim(block, layer, 0, keepdims=False)
    sent = block.astype(jnp.bfloat16)
    for k in range(1, high):
        term = lax.dynamic_index_in_dim(sent, layer ^ k, 0, keepdims=False)
        total = total + xor_permute(term, "seq", low * k).astype(jnp.float32)
    return total


def cluster_grad(query_part, key_part, live_keys):
    query_rows = query_part[:, :HD]
    grad_rows = query_part[:, HD:]
    key_rows = key_part[:, :HD]
    value_rows = key_part[:, HD:]
    scores = jnp.dot(query_rows, key_rows.T, preferred_element_type=jnp.float32) * SCALE
    scores = jnp.where(live_keys[None, :] > 0, scores, jnp.float32(-1e30))
    row_max = jnp.max(scores, axis=1, keepdims=True)
    weights = jnp.exp(scores - row_max)
    probs = weights / jnp.sum(weights, axis=1, keepdims=True)
    prob_grad = jnp.dot(grad_rows, value_rows.T, preferred_element_type=jnp.float32)
    row_dot = jnp.sum(probs * prob_grad, axis=1, keepdims=True)
    score_grad = (probs * (prob_grad - row_dot) * SCALE).astype(jnp.bfloat16)
    return jnp.dot(score_grad, key_rows, preferred_element_type=jnp.float32).astype(jnp.bfloat16)


def routed(tokens_in, queries, key_value, out_grad, cluster_of, slot_of):
    groups = lax.axis_size("seq")
    tok_count = queries.shape[0]
    row_count = tok_count * H
    bound_rows = 2 * row_count // groups
    slot_count = CL_DEV * HALF
    owners = (cluster_of // CL_DEV).reshape(row_count)
    local_slot = (cluster_of % CL_DEV * HALF + slot_of % HALF).reshape(row_count)
    picked = (owners[:, None] == jnp.arange(groups, dtype=jnp.int32)[None, :]).astype(jnp.int32)
    ranked = jnp.sum(jnp.cumsum(picked, axis=0) * picked, axis=1) - 1
    cell_index = owners * bound_rows + ranked
    paired_rows = jnp.concatenate(
        [queries.reshape(row_count, HD), out_grad.reshape(row_count, HD)], axis=1
    )
    packed = jnp.concatenate([paired_rows, jnp.repeat(key_value, H, axis=0)], axis=1)
    outgoing = jnp.zeros((groups * bound_rows, 4 * HD), jnp.bfloat16).at[cell_index].set(packed)
    labels = jnp.full((groups * bound_rows,), -1, jnp.int32).at[cell_index].set(local_slot)
    incoming = lax.all_to_all(
        outgoing.reshape(groups, bound_rows, 4 * HD), "seq", 0, 0, tiled=True
    )
    labels_in = lax.all_to_all(labels.reshape(groups, bound_rows), "seq", 0, 0, tiled=True)
    target = labels_in.reshape(groups * bound_rows)
    target_safe = jnp.where(target >= 0, target, slot_count)
    arranged = (
        jnp.zeros((slot_count, 4 * HD), jnp.bfloat16)
        .at[target_safe]
        .set(incoming.reshape(groups * bound_rows, 4 * HD), mode="drop")
    )
    live_slot = (
        jnp.zeros((slot_count,), jnp.bfloat16)
        .at[target_safe]
        .set(jnp.ones((groups * bound_rows,), jnp.bfloat16), mode="drop")
    )
    arranged = arranged.reshape(CL_DEV, HALF, 4 * HD)
    keys_all = lax.all_gather(arranged[:, :, 2 * HD :], "pair", axis=1, tiled=True)
    live_all = lax.all_gather(live_slot.reshape(CL_DEV, HALF), "pair", axis=1, tiled=True)
    cluster_grads = lax.map(
        lambda ops: cluster_grad(*ops), (arranged[:, :, : 2 * HD], keys_all, live_all)
    )
    slot_grads = cluster_grads.reshape(slot_count, HD)
    going_back = jnp.where(
        target[:, None] >= 0,
        slot_grads[jnp.minimum(target_safe, slot_count - 1)],
        jnp.zeros((), jnp.bfloat16),
    )
    returned = lax.all_to_all(
        going_back.reshape(groups, bound_rows // 2, 2 * HD), "seq", 0, 0, tiled=True
    )
    query_grad = returned.reshape(groups * bound_rows, HD)[cell_index].reshape(tok_count, H * HD)
    partial_rows = lax.psum_scatter(
        lax.dot_general(
            tokens_in, query_grad, (((0,), (0,)), ((), ())), preferred_element_type=jnp.float32
        ),
        "seq",
        scatter_dimension=0,
        tiled=True,
    )
    return lax.psum_scatter(partial_rows, "pair", scatter_dimension=0, tiled=True)


def solution(mesh):
    n = mesh.shape["seq"]
    small = n * CL_DEV == 2 * HD and n & (n - 1) == 0
    spec = P(("seq", "pair"), None)
    return jax.shard_map(
        dense if small else routed,
        mesh=mesh,
        in_specs=(spec,) * 6,
        out_specs=spec,
        check_vma=False,
    )
```

```python
import jax
import jax.numpy as jnp
from jax import lax
from jax.experimental import pallas as pl
from jax.experimental.pallas import tpu as pltpu
from jax.sharding import PartitionSpec as P

H = 16
HD = 64
HALF = 512
CL_DEV = 8
SCALE = HD ** (-0.5)
LOG2E = 1.4426950408889634
TILE = 512
LAG = 1
LATE = 0.5
UNITS = 8


def prepare_rows_kernel(q_ref, g_ref, cl_ref, left, grd):
    tok, width = q_ref.shape
    lanes = 2 * HD
    ids = lax.broadcasted_iota(jnp.int32, (lanes, tok), 0)
    for i in range(width // lanes):
        two = slice(i * lanes, (i + 1) * lanes)
        qt = (q_ref[:, two].astype(jnp.float32) * SCALE).T.astype(jnp.bfloat16)
        gt = g_ref[:, two].astype(jnp.float32).T.astype(jnp.bfloat16)
        for odd in range(2):
            h = 2 * i + odd
            half = slice(odd * HD, (odd + 1) * HD)
            mine = cl_ref[h : h + 1, :]
            hot = jnp.where(ids == mine, 1.0, 0.0).astype(jnp.bfloat16)
            same = jnp.where(ids[:HD] == jnp.bitwise_and(mine, HD - 1), 1.0, 0.0)
            left[h, 0:HD, :] = qt[half]
            left[h, HD : HD + lanes, :] = hot
            left[h, HD + lanes :, :] = same.astype(jnp.bfloat16)
            grd[h, 0:HD, :] = jnp.zeros((HD, tok), jnp.bfloat16)
            grd[h, HD:, :] = gt[half]


def prepare_rows(queries, out_grad, cluster_of):
    tok, width = queries.shape
    heads = width // HD
    return pl.pallas_call(
        prepare_rows_kernel,
        out_shape=(
            jax.ShapeDtypeStruct((heads, 4 * HD, tok), jnp.bfloat16),
            jax.ShapeDtypeStruct((heads, 2 * HD, tok), jnp.bfloat16),
        ),
        compiler_params=pltpu.CompilerParams(vmem_limit_bytes=8 * 1024 * 1024),
        cost_estimate=pl.CostEstimate(flops=10**7, bytes_accessed=2 * 10**6, transcendentals=0),
    )(queries, out_grad, cluster_of.T)


def prepare_keys_kernel(*refs):
    kv_refs = refs[:-3]
    wide, key, turned = refs[-3:]
    tok = turned.shape[2]
    lanes = 2 * HD
    quarter = HD // 2
    ids = lax.broadcasted_iota(jnp.int32, (quarter, tok), 0)
    low = lax.broadcasted_iota(jnp.int32, (tok, lanes), 1) < HD
    at = 0
    for kv_ref in kv_refs:
        for j in range(kv_ref.shape[0]):
            rows = slice(at * tok, (at + 1) * tok)
            kv = kv_ref[j, 0:tok, :]
            kv32 = kv.astype(jnp.float32)
            key[rows, :] = kv
            turned[at, :, :] = kv32.T[:HD].astype(jnp.bfloat16)
            cl = kv_ref[j, tok : tok + H, :].astype(jnp.float32).astype(jnp.int32)
            group = jnp.bitwise_and(cl, quarter - 1)
            one = jnp.left_shift(1, 8 * jnp.right_shift(cl, 5))
            packed = jnp.zeros((quarter, tok), jnp.int32)
            for h in range(H):
                packed += jnp.where(group[h : h + 1, :] == ids, one[h : h + 1, :], 0)
            res, high = [], []
            for part in range(4):
                count = jnp.bitwise_and(jnp.right_shift(packed, 8 * part), 255)
                live = count > 0
                log = jnp.log(count.astype(jnp.float32))
                hi = jnp.where(live, log, -1e30).astype(jnp.bfloat16).astype(jnp.float32)
                high.append(hi)
                res.append(jnp.where(live, log - hi, 0.0))
            small = []
            for part in range(2):
                a, b = res[part], res[part + 2]
                small.append(jnp.where(a == 0.0, b, jnp.where(b == 0.0, a, 0.5 * (a + b))))
            one = jnp.concatenate([high[0], high[1], high[0], high[1]], axis=0).T
            two = jnp.concatenate([high[2], high[3], small[0], small[1]], axis=0).T
            wide[0, rows, :] = jnp.where(low, kv32, one).astype(jnp.bfloat16)
            wide[1, rows, :] = two.astype(jnp.bfloat16)
            at += 1


def prepare_keys(gathered):
    tok = gathered[0].shape[2]
    blocks = sum(g.shape[0] for g in gathered)
    return pl.pallas_call(
        prepare_keys_kernel,
        out_shape=(
            jax.ShapeDtypeStruct((2, blocks * tok, 2 * HD), jnp.bfloat16),
            jax.ShapeDtypeStruct((blocks * tok, 2 * HD), jnp.bfloat16),
            jax.ShapeDtypeStruct((blocks, HD, tok), jnp.bfloat16),
        ),
        compiler_params=pltpu.CompilerParams(vmem_limit_bytes=8 * 1024 * 1024),
        cost_estimate=pl.CostEstimate(
            flops=blocks * 10**6, bytes_accessed=blocks * 10**5, transcendentals=0
        ),
    )(*gathered)


def attend_kernel(left, grd, *refs):
    count = (len(refs) - 10) // 3
    groups = [refs[3 * i : 3 * i + 3] for i in range(count)]
    out_ref, sc0, sc1, pg0, pg1, ds0, ds1, tp0, tp1, acc = refs[3 * count :]
    sc, pg, ds, tp = (sc0, sc1), (pg0, pg1), (ds0, ds1), (tp0, tp1)
    lanes = 2 * HD
    tok = out_ref.shape[0]
    rows = sc0.shape[1]
    per = TILE // tok
    places = [(g, j) for g, group in enumerate(groups) for j in range(group[2].shape[0] // per)]
    tiles = len(places)
    steps = out_ref.shape[1] // lanes
    unit = TILE // UNITS
    spread = (unit // 8, 8, rows)

    def tied(x, gate):
        if gate is None:
            return x
        tie = jnp.tile((gate * 0.0).astype(x.dtype), (1, x.shape[1] // gate.shape[1]))
        return jnp.concatenate([x[0:16] + tie, x[16:]], axis=0)

    def score(step, slot, t, gate):
        g, j = places[t]
        span = slice(j * TILE, (j + 1) * TILE)
        at = slice(t * TILE, (t + 1) * TILE)
        right = jnp.concatenate([left[2 * step], left[2 * step + 1]], axis=1)
        wide = jnp.concatenate([groups[g][0][0, span, :], groups[g][0][1, span, :]], axis=1)
        s = jnp.dot(wide, tied(right, gate), preferred_element_type=jnp.float32)
        sc[slot][at, :] = s
        top = jnp.max(s.reshape(TILE // 8, 8, rows), axis=0)
        tp[slot][...] = top if t == 0 else jnp.maximum(tp[slot][...], top)
        right = jnp.concatenate([grd[2 * step], grd[2 * step + 1]], axis=1)
        pg[slot][at, :] = jnp.dot(
            groups[g][1][span, :], tied(right, gate), preferred_element_type=jnp.float32
        )

    def collect(slot, t, gate):
        g, j = places[t]
        at = slice(t * TILE, (t + 1) * TILE)
        turned = jnp.concatenate([groups[g][2][j * per + b] for b in range(per)], axis=1)
        right = jnp.concatenate([ds[slot][0, at, :], ds[slot][1, at, :]], axis=1)
        add = jnp.dot(turned, tied(right, gate), preferred_element_type=jnp.float32)
        acc[...] = add if t == 0 else acc[...] + add

    def weigh(slot, u, top):
        at = slice(u * unit, (u + 1) * unit)
        w = jnp.exp(sc[slot][at, :].reshape(spread) - top)
        sc[slot][at, :] = w.reshape(unit, rows)
        wp = w * pg[slot][at, :].reshape(spread)
        return jnp.sum(w, axis=0), jnp.sum(wp, axis=0)

    def differ(slot, u, inv, dot):
        at = slice(u * unit, (u + 1) * unit)
        w = sc[slot][at, :].reshape(spread)
        d = (w * inv) * (pg[slot][at, :].reshape(spread) - dot)
        d = d.reshape(unit, rows)
        low = d.astype(jnp.bfloat16)
        for b in range(rows // lanes):
            ds[slot][b, at, :] = low[:, b * lanes : (b + 1) * lanes]
        return d[0:8, 0:lanes]

    def finish(step):
        both = jnp.concatenate([acc[:, b * lanes : (b + 1) * lanes] for b in range(2)], axis=0)
        where = pl.multiple_of(step * lanes, lanes)
        out_ref[:, pl.ds(where, lanes)] = both.T.astype(jnp.bfloat16)

    def stage(step, slot, following):
        units = tiles * UNITS
        work = [("w", u) for u in range(units)] + [("d", u) for u in range(units)]
        cost = [6.0 if kind == "w" else 4.0 for kind, _ in work]
        top = jnp.broadcast_to(jnp.max(tp[slot][...], axis=0, keepdims=True), (8, rows))[None]
        denom = jnp.zeros((8, rows), jnp.float32)
        dots = jnp.zeros((8, rows), jnp.float32)
        inv = dot = None
        gates, done, at = [None] * LAG, 0.0, 0
        for t in range(tiles):
            score(following, 1 - slot, t, gates[t])
            collect(1 - slot, t, gates[t])
            gate = None
            while at < len(work) and (t + 1 == tiles or done < sum(cost) * (t + 1) / (tiles + LATE)):
                kind, u = work[at]
                if kind == "w":
                    a, b = weigh(slot, u, top)
                    denom, dots = denom + a, dots + b
                    gate = denom[:, :lanes]
                else:
                    if inv is None:
                        whole = jnp.sum(denom, axis=0, keepdims=True)
                        dot = jnp.sum(dots, axis=0, keepdims=True) / whole
                        inv = jnp.broadcast_to(SCALE / whole, (8, rows))[None]
                        dot = jnp.broadcast_to(dot, (8, rows))[None]
                    one = differ(slot, u, inv, dot)
                    gate = one if gate is None else gate + one
                done += cost[at]
                at += 1
            gates.append(jnp.concatenate([gate, gate], axis=0))

        @pl.when(step > 0)
        def _():
            finish(step - 1)

    for t in range(tiles):
        score(0, 0, t, None)

    def body(i, _):
        stage(2 * i, 0, 2 * i + 1)
        stage(2 * i + 1, 1, jnp.minimum(2 * i + 2, steps - 1))
        return 0

    lax.fori_loop(0, steps // 2, body, 0)
    for t in range(tiles):
        collect(1, t, None)
    finish(steps - 1)


def attend(rows_of, groups, tok):
    left, grd = rows_of
    heads = left.shape[0]
    total = sum(g[1].shape[0] for g in groups)
    lanes = 2 * HD
    rows = 2 * tok
    operands = [left, grd] + [x for g in groups for x in g]
    work = heads * tok * total
    return pl.pallas_call(
        attend_kernel,
        in_specs=[pl.BlockSpec(memory_space=pltpu.VMEM)] * len(operands),
        out_specs=pl.BlockSpec(memory_space=pltpu.VMEM),
        out_shape=jax.ShapeDtypeStruct((tok, heads * HD), jnp.bfloat16),
        scratch_shapes=[pltpu.VMEM((total, rows), jnp.float32)] * 4
        + [pltpu.VMEM((rows // lanes, total, lanes), jnp.bfloat16)] * 2
        + [pltpu.VMEM((8, rows), jnp.float32)] * 2
        + [pltpu.VMEM((HD, rows), jnp.float32)],
        compiler_params=pltpu.CompilerParams(vmem_limit_bytes=40 * 1024 * 1024),
        cost_estimate=pl.CostEstimate(
            flops=work * 6 * HD, bytes_accessed=10**7, transcendentals=work
        ),
    )(*operands)


def bench(q, g, c, *parts):
    groups = [prepare_keys(parts[:1]), prepare_keys(parts[1:4]), prepare_keys(parts[4:])]
    return attend(prepare_rows(q, g, c), groups, q.shape[0])


def xor_permute(x, axis, mask):
    n = lax.axis_size(axis)
    return lax.ppermute(x, axis, [(i, i ^ mask) for i in range(n)])


def dense(tokens_in, queries, key_value, out_grad, cluster_of, slot_of):
    n = lax.axis_size("seq")
    tok, width = queries.shape
    depth = tokens_in.shape[1]
    me = lax.axis_index("pair")
    low = 1
    while low * low < n:
        low *= 2
    high = n // low
    part, layer = lax.axis_index("seq") % low, lax.axis_index("seq") // low
    piece = depth // (2 * n)
    tie = lax.optimization_barrier

    own = jnp.concatenate([key_value, cluster_of.T.astype(jnp.bfloat16)], axis=0)[None]
    above = [xor_permute(own, "seq", low * k) for k in range(1, high)]
    left = prepare_rows(queries, out_grad, cluster_of)
    x5 = tokens_in.reshape(tok, high, low, 2, piece).transpose(2, 3, 0, 1, 4)
    x5 = x5.reshape(low, 2, tok, high * piece)
    above[-1], left, x5 = tie((above[-1], left, x5))
    column = jnp.concatenate([own] + above)
    near = [xor_permute(column, "seq", k) for k in range(1, low)]
    first = prepare_keys([column])
    near[-1], first = tie((near[-1], first))
    far = [xor_permute(p, "pair", 1) for p in [column] + near]
    second = prepare_keys(near)
    far[-1], second = tie((far[-1], second))
    groups = [first, second, prepare_keys(far)]

    x_part = [lax.dynamic_index_in_dim(x5, part ^ k, 0, keepdims=False) for k in range(low)]
    x_part = [x_part[0]] + [xor_permute(x_part[k], "seq", k) for k in range(1, low)]
    x_part = jnp.stack(x_part)
    x_mine = lax.dynamic_index_in_dim(x_part, me, 1, keepdims=False)
    x_pair = xor_permute(lax.dynamic_index_in_dim(x_part, 1 - me, 1, keepdims=False), "pair", 1)

    mine = attend(left, groups, tok)

    def product(x, grad):
        return lax.dot_general(
            x, grad, (((0,), (0,)), ((), ())), preferred_element_type=jnp.float32
        )

    grads = [mine] + [xor_permute(mine, "seq", k) for k in range(1, low)]
    pairs = [xor_permute(mine, "pair", 1)]
    block = product(x_mine[0], mine) + product(x_pair[0], pairs[0])
    grads[1], block = tie((grads[1], block))
    pairs += [xor_permute(g, "pair", 1) for g in grads[1:]]
    for k in range(1, low):
        block = block + product(x_mine[k], grads[k])
    for k in range(1, low):
        block = block + product(x_pair[k], pairs[k])
    block = block.reshape(high, piece, width)
    total = lax.dynamic_index_in_dim(block, layer, 0, keepdims=False)
    sent = block.astype(jnp.bfloat16)
    for k in range(1, high):
        term = lax.dynamic_index_in_dim(sent, layer ^ k, 0, keepdims=False)
        total = total + xor_permute(term, "seq", low * k).astype(jnp.float32)
    return total


def cluster_grad(query_part, key_part, live_keys):
    query_rows = query_part[:, :HD]
    grad_rows = query_part[:, HD:]
    key_rows = key_part[:, :HD]
    value_rows = key_part[:, HD:]
    scores = jnp.dot(query_rows, key_rows.T, preferred_element_type=jnp.float32) * SCALE
    scores = jnp.where(live_keys[None, :] > 0, scores, jnp.float32(-1e30))
    row_max = jnp.max(scores, axis=1, keepdims=True)
    weights = jnp.exp(scores - row_max)
    probs = weights / jnp.sum(weights, axis=1, keepdims=True)
    prob_grad = jnp.dot(grad_rows, value_rows.T, preferred_element_type=jnp.float32)
    row_dot = jnp.sum(probs * prob_grad, axis=1, keepdims=True)
    score_grad = (probs * (prob_grad - row_dot) * SCALE).astype(jnp.bfloat16)
    return jnp.dot(score_grad, key_rows, preferred_element_type=jnp.float32).astype(jnp.bfloat16)


def routed(tokens_in, queries, key_value, out_grad, cluster_of, slot_of):
    groups = lax.axis_size("seq")
    tok_count = queries.shape[0]
    row_count = tok_count * H
    bound_rows = 2 * row_count // groups
    slot_count = CL_DEV * HALF
    owners = (cluster_of // CL_DEV).reshape(row_count)
    local_slot = (cluster_of % CL_DEV * HALF + slot_of % HALF).reshape(row_count)
    picked = (owners[:, None] == jnp.arange(groups, dtype=jnp.int32)[None, :]).astype(jnp.int32)
    ranked = jnp.sum(jnp.cumsum(picked, axis=0) * picked, axis=1) - 1
    cell_index = owners * bound_rows + ranked
    paired_rows = jnp.concatenate(
        [queries.reshape(row_count, HD), out_grad.reshape(row_count, HD)], axis=1
    )
    packed = jnp.concatenate([paired_rows, jnp.repeat(key_value, H, axis=0)], axis=1)
    outgoing = jnp.zeros((groups * bound_rows, 4 * HD), jnp.bfloat16).at[cell_index].set(packed)
    labels = jnp.full((groups * bound_rows,), -1, jnp.int32).at[cell_index].set(local_slot)
    incoming = lax.all_to_all(
        outgoing.reshape(groups, bound_rows, 4 * HD), "seq", 0, 0, tiled=True
    )
    labels_in = lax.all_to_all(labels.reshape(groups, bound_rows), "seq", 0, 0, tiled=True)
    target = labels_in.reshape(groups * bound_rows)
    target_safe = jnp.where(target >= 0, target, slot_count)
    arranged = (
        jnp.zeros((slot_count, 4 * HD), jnp.bfloat16)
        .at[target_safe]
        .set(incoming.reshape(groups * bound_rows, 4 * HD), mode="drop")
    )
    live_slot = (
        jnp.zeros((slot_count,), jnp.bfloat16)
        .at[target_safe]
        .set(jnp.ones((groups * bound_rows,), jnp.bfloat16), mode="drop")
    )
    arranged = arranged.reshape(CL_DEV, HALF, 4 * HD)
    keys_all = lax.all_gather(arranged[:, :, 2 * HD :], "pair", axis=1, tiled=True)
    live_all = lax.all_gather(live_slot.reshape(CL_DEV, HALF), "pair", axis=1, tiled=True)
    cluster_grads = lax.map(
        lambda ops: cluster_grad(*ops), (arranged[:, :, : 2 * HD], keys_all, live_all)
    )
    slot_grads = cluster_grads.reshape(slot_count, HD)
    going_back = jnp.where(
        target[:, None] >= 0,
        slot_grads[jnp.minimum(target_safe, slot_count - 1)],
        jnp.zeros((), jnp.bfloat16),
    )
    returned = lax.all_to_all(
        going_back.reshape(groups, bound_rows // 2, 2 * HD), "seq", 0, 0, tiled=True
    )
    query_grad = returned.reshape(groups * bound_rows, HD)[cell_index].reshape(tok_count, H * HD)
    partial_rows = lax.psum_scatter(
        lax.dot_general(
            tokens_in, query_grad, (((0,), (0,)), ((), ())), preferred_element_type=jnp.float32
        ),
        "seq",
        scatter_dimension=0,
        tiled=True,
    )
    return lax.psum_scatter(partial_rows, "pair", scatter_dimension=0, tiled=True)


def solution(mesh):
    n = mesh.shape["seq"]
    small = n * CL_DEV == 2 * HD and n & (n - 1) == 0
    spec = P(("seq", "pair"), None)
    return jax.shard_map(
        dense if small else routed,
        mesh=mesh,
        in_specs=(spec,) * 6,
        out_specs=spec,
        check_vma=False,
    )
```

```python
import jax
import jax.numpy as jnp
from jax import lax
from jax.experimental import pallas as pl
from jax.experimental.pallas import tpu as pltpu
from jax.sharding import PartitionSpec as P


H = 16
HD = 64
HALF = 512
CL_DEV = 8
SCALE = HD ** (-0.5)
TILE = 512
LAG = 1
LATE = 0.5
UNITS = 8


def prepare_rows_kernel(q_ref, g_ref, cl_ref, left, grd):
    tok, width = q_ref.shape
    lanes = 2 * HD
    ids = lax.broadcasted_iota(jnp.int32, (lanes, tok), 0)
    for i in range(width // lanes):
        two = slice(i * lanes, (i + 1) * lanes)
        qt = (q_ref[:, two].astype(jnp.float32) * SCALE).T.astype(jnp.bfloat16)
        gt = g_ref[:, two].astype(jnp.float32).T.astype(jnp.bfloat16)
        for odd in range(2):
            h = 2 * i + odd
            half = slice(odd * HD, (odd + 1) * HD)
            mine = cl_ref[h : h + 1, :]
            hot = jnp.where(ids == mine, 1.0, 0.0).astype(jnp.bfloat16)
            same = jnp.where(ids[:HD] == jnp.bitwise_and(mine, HD - 1), 1.0, 0.0)
            left[h, 0:HD, :] = qt[half]
            left[h, HD : HD + lanes, :] = hot
            left[h, HD + lanes :, :] = same.astype(jnp.bfloat16)
            grd[h, 0:HD, :] = jnp.zeros((HD, tok), jnp.bfloat16)
            grd[h, HD:, :] = gt[half]


def prepare_rows(queries, out_grad, cluster_of):
    tok, width = queries.shape
    heads = width // HD
    return pl.pallas_call(
        prepare_rows_kernel,
        out_shape=(
            jax.ShapeDtypeStruct((heads, 4 * HD, tok), jnp.bfloat16),
            jax.ShapeDtypeStruct((heads, 2 * HD, tok), jnp.bfloat16),
        ),
        compiler_params=pltpu.CompilerParams(vmem_limit_bytes=8 * 1024 * 1024),
        cost_estimate=pl.CostEstimate(flops=10**7, bytes_accessed=2 * 10**6, transcendentals=0),
    )(queries, out_grad, cluster_of.T)


def prepare_keys_kernel(*refs):
    kv_refs = refs[:-3]
    wide, key, turned = refs[-3:]
    tok = turned.shape[2]
    lanes = 2 * HD
    quarter = HD // 2
    ids = lax.broadcasted_iota(jnp.int32, (quarter, tok), 0)
    low = lax.broadcasted_iota(jnp.int32, (tok, lanes), 1) < HD
    at = 0
    for kv_ref in kv_refs:
        for j in range(kv_ref.shape[0]):
            rows = slice(at * tok, (at + 1) * tok)
            kv = kv_ref[j, 0:tok, :]
            kv32 = kv.astype(jnp.float32)
            key[rows, :] = kv
            turned[at, :, :] = kv32.T[:HD].astype(jnp.bfloat16)
            cl = kv_ref[j, tok : tok + H, :].astype(jnp.float32).astype(jnp.int32)
            group = jnp.bitwise_and(cl, quarter - 1)
            one = jnp.left_shift(1, 8 * jnp.right_shift(cl, 5))
            packed = jnp.zeros((quarter, tok), jnp.int32)
            for h in range(H):
                packed += jnp.where(group[h : h + 1, :] == ids, one[h : h + 1, :], 0)
            res, high = [], []
            for part in range(4):
                count = jnp.bitwise_and(jnp.right_shift(packed, 8 * part), 255)
                live = count > 0
                log = jnp.log(count.astype(jnp.float32))
                hi = jnp.where(live, log, -1e30).astype(jnp.bfloat16).astype(jnp.float32)
                high.append(hi)
                res.append(jnp.where(live, log - hi, 0.0))
            small = []
            for part in range(2):
                a, b = res[part], res[part + 2]
                small.append(jnp.where(a == 0.0, b, jnp.where(b == 0.0, a, 0.5 * (a + b))))
            one = jnp.concatenate([high[0], high[1], high[0], high[1]], axis=0).T
            two = jnp.concatenate([high[2], high[3], small[0], small[1]], axis=0).T
            wide[0, rows, :] = jnp.where(low, kv32, one).astype(jnp.bfloat16)
            wide[1, rows, :] = two.astype(jnp.bfloat16)
            at += 1


def prepare_keys(gathered):
    tok = gathered[0].shape[2]
    blocks = sum(g.shape[0] for g in gathered)
    return pl.pallas_call(
        prepare_keys_kernel,
        out_shape=(
            jax.ShapeDtypeStruct((2, blocks * tok, 2 * HD), jnp.bfloat16),
            jax.ShapeDtypeStruct((blocks * tok, 2 * HD), jnp.bfloat16),
            jax.ShapeDtypeStruct((blocks, HD, tok), jnp.bfloat16),
        ),
        compiler_params=pltpu.CompilerParams(vmem_limit_bytes=8 * 1024 * 1024),
        cost_estimate=pl.CostEstimate(
            flops=blocks * 10**6, bytes_accessed=blocks * 10**5, transcendentals=0
        ),
    )(*gathered)


def attend_kernel(left, grd, *refs):
    count = (len(refs) - 10) // 3
    groups = [refs[3 * i : 3 * i + 3] for i in range(count)]
    out_ref, sc0, sc1, pg0, pg1, ds0, ds1, tp0, tp1, acc = refs[3 * count :]
    sc, pg, ds, tp = (sc0, sc1), (pg0, pg1), (ds0, ds1), (tp0, tp1)
    lanes = 2 * HD
    tok = out_ref.shape[0]
    rows = sc0.shape[1]
    per = TILE // tok
    places = [(g, j) for g, group in enumerate(groups) for j in range(group[2].shape[0] // per)]
    tiles = len(places)
    steps = out_ref.shape[1] // lanes
    unit = TILE // UNITS
    spread = (unit // 8, 8, rows)

    def tied(x, gate):
        if gate is None:
            return x
        tie = jnp.tile((gate * 0.0).astype(x.dtype), (1, x.shape[1] // gate.shape[1]))
        return jnp.concatenate([x[0:16] + tie, x[16:]], axis=0)

    def score(step, slot, t, gate):
        g, j = places[t]
        span = slice(j * TILE, (j + 1) * TILE)
        at = slice(t * TILE, (t + 1) * TILE)
        right = jnp.concatenate([left[2 * step], left[2 * step + 1]], axis=1)
        wide = jnp.concatenate([groups[g][0][0, span, :], groups[g][0][1, span, :]], axis=1)
        s = jnp.dot(wide, tied(right, gate), preferred_element_type=jnp.float32)
        sc[slot][at, :] = s
        top = jnp.max(s.reshape(TILE // 8, 8, rows), axis=0)
        tp[slot][...] = top if t == 0 else jnp.maximum(tp[slot][...], top)
        right = jnp.concatenate([grd[2 * step], grd[2 * step + 1]], axis=1)
        pg[slot][at, :] = jnp.dot(
            groups[g][1][span, :], tied(right, gate), preferred_element_type=jnp.float32
        )

    def collect(slot, t, gate):
        g, j = places[t]
        at = slice(t * TILE, (t + 1) * TILE)
        turned = jnp.concatenate([groups[g][2][j * per + b] for b in range(per)], axis=1)
        right = jnp.concatenate([ds[slot][0, at, :], ds[slot][1, at, :]], axis=1)
        add = jnp.dot(turned, tied(right, gate), preferred_element_type=jnp.float32)
        acc[...] = add if t == 0 else acc[...] + add

    def weigh(slot, u, top):
        at = slice(u * unit, (u + 1) * unit)
        w = jnp.exp(sc[slot][at, :].reshape(spread) - top)
        sc[slot][at, :] = w.reshape(unit, rows)
        wp = w * pg[slot][at, :].reshape(spread)
        return jnp.sum(w, axis=0), jnp.sum(wp, axis=0)

    def differ(slot, u, inv, dot):
        at = slice(u * unit, (u + 1) * unit)
        w = sc[slot][at, :].reshape(spread)
        d = (w * inv) * (pg[slot][at, :].reshape(spread) - dot)
        d = d.reshape(unit, rows)
        low = d.astype(jnp.bfloat16)
        for b in range(rows // lanes):
            ds[slot][b, at, :] = low[:, b * lanes : (b + 1) * lanes]
        return d[0:8, 0:lanes]

    def finish(step):
        both = jnp.concatenate([acc[:, b * lanes : (b + 1) * lanes] for b in range(2)], axis=0)
        where = pl.multiple_of(step * lanes, lanes)
        out_ref[:, pl.ds(where, lanes)] = both.T.astype(jnp.bfloat16)

    def stage(step, slot, following):
        units = tiles * UNITS
        work = [("w", u) for u in range(units)] + [("d", u) for u in range(units)]
        cost = [6.0 if kind == "w" else 4.0 for kind, _ in work]
        top = jnp.broadcast_to(jnp.max(tp[slot][...], axis=0, keepdims=True), (8, rows))[None]
        denom = jnp.zeros((8, rows), jnp.float32)
        dots = jnp.zeros((8, rows), jnp.float32)
        inv = dot = None
        gates, done, at = [None] * LAG, 0.0, 0
        for t in range(tiles):
            score(following, 1 - slot, t, gates[t])
            collect(1 - slot, t, gates[t])
            gate = None
            while at < len(work) and (t + 1 == tiles or done < sum(cost) * (t + 1) / (tiles + LATE)):
                kind, u = work[at]
                if kind == "w":
                    a, b = weigh(slot, u, top)
                    denom, dots = denom + a, dots + b
                    gate = denom[:, :lanes]
                else:
                    if inv is None:
                        whole = jnp.sum(denom, axis=0, keepdims=True)
                        dot = jnp.sum(dots, axis=0, keepdims=True) / whole
                        inv = jnp.broadcast_to(SCALE / whole, (8, rows))[None]
                        dot = jnp.broadcast_to(dot, (8, rows))[None]
                    one = differ(slot, u, inv, dot)
                    gate = one if gate is None else gate + one
                done += cost[at]
                at += 1
            gates.append(jnp.concatenate([gate, gate], axis=0))

        @pl.when(step > 0)
        def _():
            finish(step - 1)

    for t in range(tiles):
        score(0, 0, t, None)

    def body(i, _):
        stage(2 * i, 0, 2 * i + 1)
        stage(2 * i + 1, 1, jnp.minimum(2 * i + 2, steps - 1))
        return 0

    lax.fori_loop(0, steps // 2, body, 0)
    for t in range(tiles):
        collect(1, t, None)
    finish(steps - 1)


def attend(rows_of, groups, tok):
    left, grd = rows_of
    heads = left.shape[0]
    total = sum(g[1].shape[0] for g in groups)
    lanes = 2 * HD
    rows = 2 * tok
    operands = [left, grd] + [x for g in groups for x in g]
    work = heads * tok * total
    return pl.pallas_call(
        attend_kernel,
        in_specs=[pl.BlockSpec(memory_space=pltpu.VMEM)] * len(operands),
        out_specs=pl.BlockSpec(memory_space=pltpu.VMEM),
        out_shape=jax.ShapeDtypeStruct((tok, heads * HD), jnp.bfloat16),
        scratch_shapes=[pltpu.VMEM((total, rows), jnp.float32)] * 4
        + [pltpu.VMEM((rows // lanes, total, lanes), jnp.bfloat16)] * 2
        + [pltpu.VMEM((8, rows), jnp.float32)] * 2
        + [pltpu.VMEM((HD, rows), jnp.float32)],
        compiler_params=pltpu.CompilerParams(vmem_limit_bytes=40 * 1024 * 1024),
        cost_estimate=pl.CostEstimate(
            flops=work * 6 * HD, bytes_accessed=10**7, transcendentals=work
        ),
    )(*operands)


def xor_permute(x, axis, mask):
    n = lax.axis_size(axis)
    return lax.ppermute(x, axis, [(i, i ^ mask) for i in range(n)])


def dense(tokens_in, queries, key_value, out_grad, cluster_of, slot_of):
    n = lax.axis_size("seq")
    tok, width = queries.shape
    depth = tokens_in.shape[1]
    me = lax.axis_index("pair")
    low = 1
    while low * low < n:
        low *= 2
    high = n // low
    part, layer = lax.axis_index("seq") % low, lax.axis_index("seq") // low
    piece = depth // (2 * n)
    tie = lax.optimization_barrier

    own = jnp.concatenate([key_value, cluster_of.T.astype(jnp.bfloat16)], axis=0)[None]
    above = [xor_permute(own, "seq", low * k) for k in range(1, high)]
    left = prepare_rows(queries, out_grad, cluster_of)
    x5 = tokens_in.reshape(tok, high, low, 2, piece).transpose(2, 3, 0, 1, 4)
    x5 = x5.reshape(low, 2, tok, high * piece)
    above[-1], left, x5 = tie((above[-1], left, x5))
    column = jnp.concatenate([own] + above)
    near = [xor_permute(column, "seq", k) for k in range(1, low)]
    first = prepare_keys([column])
    near[-1], first = tie((near[-1], first))
    far = [xor_permute(p, "pair", 1) for p in [column] + near]
    second = prepare_keys(near)
    far[-1], second = tie((far[-1], second))
    groups = [first, second, prepare_keys(far)]

    x_part = [lax.dynamic_index_in_dim(x5, part ^ k, 0, keepdims=False) for k in range(low)]
    x_part = [x_part[0]] + [xor_permute(x_part[k], "seq", k) for k in range(1, low)]
    x_part = jnp.stack(x_part)
    x_mine = lax.dynamic_index_in_dim(x_part, me, 1, keepdims=False)
    x_pair = lax.dynamic_index_in_dim(x_part, 1 - me, 1, keepdims=False)
    x_pair = xor_permute(x_pair, "pair", 1)

    mine = attend(left, groups, tok)

    def product(x, grad):
        return lax.dot_general(
            x, grad, (((0,), (0,)), ((), ())), preferred_element_type=jnp.float32
        )

    grads = [mine] + [xor_permute(mine, "seq", k) for k in range(1, low)]
    pairs = [xor_permute(mine, "pair", 1)]
    block = product(x_mine[0], mine) + product(x_pair[0], pairs[0])
    grads[1], block = tie((grads[1], block))
    pairs += [xor_permute(g, "pair", 1) for g in grads[1:]]
    for k in range(1, low):
        block = block + product(x_mine[k], grads[k])
    for k in range(1, low):
        block = block + product(x_pair[k], pairs[k])
    block = block.reshape(high, piece, width)
    total = lax.dynamic_index_in_dim(block, layer, 0, keepdims=False)
    sent = block.astype(jnp.bfloat16)
    for k in range(1, high):
        term = lax.dynamic_index_in_dim(sent, layer ^ k, 0, keepdims=False)
        total = total + xor_permute(term, "seq", low * k).astype(jnp.float32)
    return total


def cluster_grad(query_part, key_part, live_keys):
    query_rows = query_part[:, :HD]
    grad_rows = query_part[:, HD:]
    key_rows = key_part[:, :HD]
    value_rows = key_part[:, HD:]
    scores = jnp.dot(query_rows, key_rows.T, preferred_element_type=jnp.float32) * SCALE
    scores = jnp.where(live_keys[None, :] > 0, scores, jnp.float32(-1e30))
    row_max = jnp.max(scores, axis=1, keepdims=True)
    weights = jnp.exp(scores - row_max)
    probs = weights / jnp.sum(weights, axis=1, keepdims=True)
    prob_grad = jnp.dot(grad_rows, value_rows.T, preferred_element_type=jnp.float32)
    row_dot = jnp.sum(probs * prob_grad, axis=1, keepdims=True)
    score_grad = (probs * (prob_grad - row_dot) * SCALE).astype(jnp.bfloat16)
    return jnp.dot(score_grad, key_rows, preferred_element_type=jnp.float32).astype(jnp.bfloat16)


def routed(tokens_in, queries, key_value, out_grad, cluster_of, slot_of):
    groups = lax.axis_size("seq")
    tok_count = queries.shape[0]
    row_count = tok_count * H
    bound_rows = 2 * row_count // groups
    slot_count = CL_DEV * HALF
    owners = (cluster_of // CL_DEV).reshape(row_count)
    local_slot = (cluster_of % CL_DEV * HALF + slot_of % HALF).reshape(row_count)
    picked = (owners[:, None] == jnp.arange(groups, dtype=jnp.int32)[None, :]).astype(jnp.int32)
    ranked = jnp.sum(jnp.cumsum(picked, axis=0) * picked, axis=1) - 1
    cell_index = owners * bound_rows + ranked
    paired_rows = jnp.concatenate(
        [queries.reshape(row_count, HD), out_grad.reshape(row_count, HD)], axis=1
    )
    packed = jnp.concatenate([paired_rows, jnp.repeat(key_value, H, axis=0)], axis=1)
    outgoing = jnp.zeros((groups * bound_rows, 4 * HD), jnp.bfloat16).at[cell_index].set(packed)
    labels = jnp.full((groups * bound_rows,), -1, jnp.int32).at[cell_index].set(local_slot)
    incoming = lax.all_to_all(
        outgoing.reshape(groups, bound_rows, 4 * HD), "seq", 0, 0, tiled=True
    )
    labels_in = lax.all_to_all(labels.reshape(groups, bound_rows), "seq", 0, 0, tiled=True)
    target = labels_in.reshape(groups * bound_rows)
    target_safe = jnp.where(target >= 0, target, slot_count)
    arranged = (
        jnp.zeros((slot_count, 4 * HD), jnp.bfloat16)
        .at[target_safe]
        .set(incoming.reshape(groups * bound_rows, 4 * HD), mode="drop")
    )
    live_slot = (
        jnp.zeros((slot_count,), jnp.bfloat16)
        .at[target_safe]
        .set(jnp.ones((groups * bound_rows,), jnp.bfloat16), mode="drop")
    )
    arranged = arranged.reshape(CL_DEV, HALF, 4 * HD)
    keys_all = lax.all_gather(arranged[:, :, 2 * HD :], "pair", axis=1, tiled=True)
    live_all = lax.all_gather(live_slot.reshape(CL_DEV, HALF), "pair", axis=1, tiled=True)
    cluster_grads = lax.map(
        lambda ops: cluster_grad(*ops), (arranged[:, :, : 2 * HD], keys_all, live_all)
    )
    slot_grads = cluster_grads.reshape(slot_count, HD)
    going_back = jnp.where(
        target[:, None] >= 0,
        slot_grads[jnp.minimum(target_safe, slot_count - 1)],
        jnp.zeros((), jnp.bfloat16),
    )
    returned = lax.all_to_all(
        going_back.reshape(groups, bound_rows // 2, 2 * HD), "seq", 0, 0, tiled=True
    )
    query_grad = returned.reshape(groups * bound_rows, HD)[cell_index].reshape(tok_count, H * HD)
    partial_rows = lax.psum_scatter(
        lax.dot_general(
            tokens_in, query_grad, (((0,), (0,)), ((), ())), preferred_element_type=jnp.float32
        ),
        "seq",
        scatter_dimension=0,
        tiled=True,
    )
    return lax.psum_scatter(partial_rows, "pair", scatter_dimension=0, tiled=True)


def solution(mesh):
    n = mesh.shape["seq"]
    small = n * CL_DEV == 2 * HD and n & (n - 1) == 0
    spec = P(("seq", "pair"), None)
    return jax.shard_map(
        dense if small else routed,
        mesh=mesh,
        in_specs=(spec,) * 6,
        out_specs=spec,
        check_vma=False,
    )
```

```python
import functools

import jax
import jax.numpy as jnp
from jax import lax
from jax.experimental import pallas as pl
from jax.experimental.pallas import tpu as pltpu
from jax.sharding import PartitionSpec as P


H = 16
HD = 64
HALF = 512
CL_DEV = 8
SCALE = HD ** (-0.5)
TILE = 512
LAG = 1
LATE = 0.5
UNITS = 8


def prepare_rows_kernel(q_ref, g_ref, cl_ref, left, grd):
    tok, width = q_ref.shape
    lanes = 2 * HD
    ids = lax.broadcasted_iota(jnp.int32, (lanes, tok), 0)
    for i in range(width // lanes):
        two = slice(i * lanes, (i + 1) * lanes)
        qt = (q_ref[:, two].astype(jnp.float32) * SCALE).T.astype(jnp.bfloat16)
        gt = g_ref[:, two].astype(jnp.float32).T.astype(jnp.bfloat16)
        for odd in range(2):
            h = 2 * i + odd
            half = slice(odd * HD, (odd + 1) * HD)
            mine = cl_ref[h : h + 1, :]
            hot = jnp.where(ids == mine, 1.0, 0.0).astype(jnp.bfloat16)
            same = jnp.where(ids[:HD] == jnp.bitwise_and(mine, HD - 1), 1.0, 0.0)
            left[h, 0:HD, :] = qt[half]
            left[h, HD : HD + lanes, :] = hot
            left[h, HD + lanes :, :] = same.astype(jnp.bfloat16)
            grd[h, 0:HD, :] = jnp.zeros((HD, tok), jnp.bfloat16)
            grd[h, HD:, :] = gt[half]


def prepare_rows(queries, out_grad, cluster_of):
    tok, width = queries.shape
    heads = width // HD
    return pl.pallas_call(
        prepare_rows_kernel,
        out_shape=(
            jax.ShapeDtypeStruct((heads, 4 * HD, tok), jnp.bfloat16),
            jax.ShapeDtypeStruct((heads, 2 * HD, tok), jnp.bfloat16),
        ),
        compiler_params=pltpu.CompilerParams(vmem_limit_bytes=8 * 1024 * 1024),
        cost_estimate=pl.CostEstimate(flops=10**7, bytes_accessed=2 * 10**6, transcendentals=0),
    )(queries, out_grad, cluster_of.T)


def prepare_keys_kernel(*refs):
    kv_refs = refs[:-3]
    wide, key, turned = refs[-3:]
    tok = turned.shape[2]
    lanes = 2 * HD
    quarter = HD // 2
    ids = lax.broadcasted_iota(jnp.int32, (quarter, tok), 0)
    low = lax.broadcasted_iota(jnp.int32, (tok, lanes), 1) < HD
    at = 0
    for kv_ref in kv_refs:
        for j in range(kv_ref.shape[0]):
            rows = slice(at * tok, (at + 1) * tok)
            kv = kv_ref[j, 0:tok, :]
            kv32 = kv.astype(jnp.float32)
            key[rows, :] = kv
            turned[at, :, :] = kv32.T[:HD].astype(jnp.bfloat16)
            cl = kv_ref[j, tok : tok + H, :].astype(jnp.float32).astype(jnp.int32)
            group = jnp.bitwise_and(cl, quarter - 1)
            one = jnp.left_shift(1, 8 * jnp.right_shift(cl, 5))
            packed = jnp.zeros((quarter, tok), jnp.int32)
            for h in range(H):
                packed += jnp.where(group[h : h + 1, :] == ids, one[h : h + 1, :], 0)
            res, high = [], []
            for part in range(4):
                count = jnp.bitwise_and(jnp.right_shift(packed, 8 * part), 255)
                live = count > 0
                log = jnp.log(count.astype(jnp.float32))
                hi = jnp.where(live, log, -1e30).astype(jnp.bfloat16).astype(jnp.float32)
                high.append(hi)
                res.append(jnp.where(live, log - hi, 0.0))
            small = []
            for part in range(2):
                a, b = res[part], res[part + 2]
                small.append(jnp.where(a == 0.0, b, jnp.where(b == 0.0, a, 0.5 * (a + b))))
            one = jnp.concatenate([high[0], high[1], high[0], high[1]], axis=0).T
            two = jnp.concatenate([high[2], high[3], small[0], small[1]], axis=0).T
            wide[0, rows, :] = jnp.where(low, kv32, one).astype(jnp.bfloat16)
            wide[1, rows, :] = two.astype(jnp.bfloat16)
            at += 1


def prepare_keys(gathered):
    tok = gathered[0].shape[2]
    blocks = sum(g.shape[0] for g in gathered)
    return pl.pallas_call(
        prepare_keys_kernel,
        out_shape=(
            jax.ShapeDtypeStruct((2, blocks * tok, 2 * HD), jnp.bfloat16),
            jax.ShapeDtypeStruct((blocks * tok, 2 * HD), jnp.bfloat16),
            jax.ShapeDtypeStruct((blocks, HD, tok), jnp.bfloat16),
        ),
        compiler_params=pltpu.CompilerParams(vmem_limit_bytes=8 * 1024 * 1024),
        cost_estimate=pl.CostEstimate(
            flops=blocks * 10**6, bytes_accessed=blocks * 10**5, transcendentals=0
        ),
    )(*gathered)


def attend_kernel(begin, left, grd, *refs):
    count = (len(refs) - 10) // 3
    groups = [refs[3 * i : 3 * i + 3] for i in range(count)]
    out_ref, sc0, sc1, pg0, pg1, ds0, ds1, tp0, tp1, acc = refs[3 * count :]
    sc, pg, ds, tp = (sc0, sc1), (pg0, pg1), (ds0, ds1), (tp0, tp1)
    lanes = 2 * HD
    tok = out_ref.shape[0]
    rows = sc0.shape[1]
    per = TILE // tok
    places = [(g, j) for g, group in enumerate(groups) for j in range(group[2].shape[0] // per)]
    tiles = len(places)
    steps = out_ref.shape[1] // lanes
    unit = TILE // UNITS
    spread = (unit // 8, 8, rows)

    def tied(x, gate):
        if gate is None:
            return x
        tie = jnp.tile((gate * 0.0).astype(x.dtype), (1, x.shape[1] // gate.shape[1]))
        return jnp.concatenate([x[0:16] + tie, x[16:]], axis=0)

    def score(step, slot, t, gate):
        g, j = places[t]
        span = slice(j * TILE, (j + 1) * TILE)
        at = slice(t * TILE, (t + 1) * TILE)
        right = jnp.concatenate([left[begin + 2 * step], left[begin + 2 * step + 1]], axis=1)
        wide = jnp.concatenate([groups[g][0][0, span, :], groups[g][0][1, span, :]], axis=1)
        s = jnp.dot(wide, tied(right, gate), preferred_element_type=jnp.float32)
        sc[slot][at, :] = s
        top = jnp.max(s.reshape(TILE // 8, 8, rows), axis=0)
        tp[slot][...] = top if t == 0 else jnp.maximum(tp[slot][...], top)
        right = jnp.concatenate([grd[begin + 2 * step], grd[begin + 2 * step + 1]], axis=1)
        pg[slot][at, :] = jnp.dot(
            groups[g][1][span, :], tied(right, gate), preferred_element_type=jnp.float32
        )

    def collect(slot, t, gate):
        g, j = places[t]
        at = slice(t * TILE, (t + 1) * TILE)
        turned = jnp.concatenate([groups[g][2][j * per + b] for b in range(per)], axis=1)
        right = jnp.concatenate([ds[slot][0, at, :], ds[slot][1, at, :]], axis=1)
        add = jnp.dot(turned, tied(right, gate), preferred_element_type=jnp.float32)
        acc[...] = add if t == 0 else acc[...] + add

    def weigh(slot, u, top):
        at = slice(u * unit, (u + 1) * unit)
        w = jnp.exp(sc[slot][at, :].reshape(spread) - top)
        sc[slot][at, :] = w.reshape(unit, rows)
        wp = w * pg[slot][at, :].reshape(spread)
        return jnp.sum(w, axis=0), jnp.sum(wp, axis=0)

    def differ(slot, u, inv, dot):
        at = slice(u * unit, (u + 1) * unit)
        w = sc[slot][at, :].reshape(spread)
        d = (w * inv) * (pg[slot][at, :].reshape(spread) - dot)
        d = d.reshape(unit, rows)
        low = d.astype(jnp.bfloat16)
        for b in range(rows // lanes):
            ds[slot][b, at, :] = low[:, b * lanes : (b + 1) * lanes]
        return d[0:8, 0:lanes]

    def finish(step):
        both = jnp.concatenate([acc[:, b * lanes : (b + 1) * lanes] for b in range(2)], axis=0)
        where = pl.multiple_of(step * lanes, lanes)
        out_ref[:, pl.ds(where, lanes)] = both.T.astype(jnp.bfloat16)

    def stage(step, slot, following):
        units = tiles * UNITS
        work = [("w", u) for u in range(units)] + [("d", u) for u in range(units)]
        cost = [6.0 if kind == "w" else 4.0 for kind, _ in work]
        top = jnp.broadcast_to(jnp.max(tp[slot][...], axis=0, keepdims=True), (8, rows))[None]
        denom = jnp.zeros((8, rows), jnp.float32)
        dots = jnp.zeros((8, rows), jnp.float32)
        inv = dot = None
        gates, done, at = [None] * LAG, 0.0, 0
        for t in range(tiles):
            score(following, 1 - slot, t, gates[t])
            collect(1 - slot, t, gates[t])
            gate = None
            while at < len(work) and (t + 1 == tiles or done < sum(cost) * (t + 1) / (tiles + LATE)):
                kind, u = work[at]
                if kind == "w":
                    a, b = weigh(slot, u, top)
                    denom, dots = denom + a, dots + b
                    gate = denom[:, :lanes]
                else:
                    if inv is None:
                        whole = jnp.sum(denom, axis=0, keepdims=True)
                        dot = jnp.sum(dots, axis=0, keepdims=True) / whole
                        inv = jnp.broadcast_to(SCALE / whole, (8, rows))[None]
                        dot = jnp.broadcast_to(dot, (8, rows))[None]
                    one = differ(slot, u, inv, dot)
                    gate = one if gate is None else gate + one
                done += cost[at]
                at += 1
            gates.append(jnp.concatenate([gate, gate], axis=0))

        @pl.when(step > 0)
        def _():
            finish(step - 1)

    for t in range(tiles):
        score(0, 0, t, None)

    def body(i, _):
        stage(2 * i, 0, 2 * i + 1)
        stage(2 * i + 1, 1, jnp.minimum(2 * i + 2, steps - 1))
        return 0

    lax.fori_loop(0, steps // 2, body, 0)
    for t in range(tiles):
        collect(1, t, None)
    finish(steps - 1)


def attend(rows_of, groups, tok, begin, heads):
    left, grd = rows_of
    total = sum(g[1].shape[0] for g in groups)
    lanes = 2 * HD
    rows = 2 * tok
    operands = [left, grd] + [x for g in groups for x in g]
    work = heads * tok * total
    return pl.pallas_call(
        functools.partial(attend_kernel, begin),
        in_specs=[pl.BlockSpec(memory_space=pltpu.VMEM)] * len(operands),
        out_specs=pl.BlockSpec(memory_space=pltpu.VMEM),
        out_shape=jax.ShapeDtypeStruct((tok, heads * HD), jnp.bfloat16),
        scratch_shapes=[pltpu.VMEM((total, rows), jnp.float32)] * 4
        + [pltpu.VMEM((rows // lanes, total, lanes), jnp.bfloat16)] * 2
        + [pltpu.VMEM((8, rows), jnp.float32)] * 2
        + [pltpu.VMEM((HD, rows), jnp.float32)],
        compiler_params=pltpu.CompilerParams(vmem_limit_bytes=40 * 1024 * 1024),
        cost_estimate=pl.CostEstimate(
            flops=work * 6 * HD, bytes_accessed=10**7, transcendentals=work
        ),
    )(*operands)


def xor_permute(x, axis, mask):
    n = lax.axis_size(axis)
    return lax.ppermute(x, axis, [(i, i ^ mask) for i in range(n)])


def dense(tokens_in, queries, key_value, out_grad, cluster_of, slot_of):
    n = lax.axis_size("seq")
    tok, width = queries.shape
    depth = tokens_in.shape[1]
    me = lax.axis_index("pair")
    low = 1
    while low * low < n:
        low *= 2
    high = n // low
    part, layer = lax.axis_index("seq") % low, lax.axis_index("seq") // low
    piece = depth // (2 * n)
    tie = lax.optimization_barrier

    own = jnp.concatenate([key_value, cluster_of.T.astype(jnp.bfloat16)], axis=0)[None]
    above = [xor_permute(own, "seq", low * k) for k in range(1, high)]
    left = prepare_rows(queries, out_grad, cluster_of)
    x5 = tokens_in.reshape(tok, high, low, 2, piece).transpose(2, 3, 0, 1, 4)
    x5 = x5.reshape(low, 2, tok, high * piece)
    above[-1], left, x5 = tie((above[-1], left, x5))
    column = jnp.concatenate([own] + above)
    near = [xor_permute(column, "seq", k) for k in range(1, low)]
    first = prepare_keys([column])
    near[-1], first = tie((near[-1], first))
    far = [xor_permute(p, "pair", 1) for p in [column] + near]
    second = prepare_keys(near)
    far[-1], second = tie((far[-1], second))
    groups = [first, second, prepare_keys(far)]

    x_part = [lax.dynamic_index_in_dim(x5, part ^ k, 0, keepdims=False) for k in range(low)]
    x_part = [x_part[0]] + [xor_permute(x_part[k], "seq", k) for k in range(1, low)]

    def product(x, grad):
        return lax.dot_general(
            x, grad, (((0,), (0,)), ((), ())), preferred_element_type=jnp.float32
        )

    def spread(grad):
        return [grad] + [xor_permute(grad, "seq", k) for k in range(1, low)]

    heads = width // HD
    cut = heads * 3 // 4
    most = spread(attend(left, groups, tok, 0, cut))
    rest = attend(left, groups, tok, cut, heads - cut)
    x_part, _ = tie((x_part, rest))
    x_part = jnp.stack(x_part)
    x_mine = lax.dynamic_index_in_dim(x_part, me, 1, keepdims=False)
    x_pair = lax.dynamic_index_in_dim(x_part, 1 - me, 1, keepdims=False)
    x_pair = xor_permute(x_pair, "pair", 1)
    rest = spread(rest)
    pairs = [xor_permute(g, "pair", 1) for g in most]
    block = sum(product(x_mine[k], most[k]) + product(x_pair[k], pairs[k]) for k in range(low))
    pairs = [xor_permute(rest[0], "pair", 1)]
    last = product(x_mine[0], rest[0]) + product(x_pair[0], pairs[0])
    rest[1:], block, last = tie((rest[1:], block, last))
    pairs += [xor_permute(g, "pair", 1) for g in rest[1:]]
    for k in range(1, low):
        last = last + product(x_mine[k], rest[k])
    for k in range(1, low):
        last = last + product(x_pair[k], pairs[k])
    block = jnp.concatenate([block, last], axis=1)
    block = block.reshape(high, piece, width)
    total = lax.dynamic_index_in_dim(block, layer, 0, keepdims=False)
    sent = block.astype(jnp.bfloat16)
    for k in range(1, high):
        term = lax.dynamic_index_in_dim(sent, layer ^ k, 0, keepdims=False)
        total = total + xor_permute(term, "seq", low * k).astype(jnp.float32)
    return total


def cluster_grad(query_part, key_part, live_keys):
    query_rows = query_part[:, :HD]
    grad_rows = query_part[:, HD:]
    key_rows = key_part[:, :HD]
    value_rows = key_part[:, HD:]
    scores = jnp.dot(query_rows, key_rows.T, preferred_element_type=jnp.float32) * SCALE
    scores = jnp.where(live_keys[None, :] > 0, scores, jnp.float32(-1e30))
    row_max = jnp.max(scores, axis=1, keepdims=True)
    weights = jnp.exp(scores - row_max)
    probs = weights / jnp.sum(weights, axis=1, keepdims=True)
    prob_grad = jnp.dot(grad_rows, value_rows.T, preferred_element_type=jnp.float32)
    row_dot = jnp.sum(probs * prob_grad, axis=1, keepdims=True)
    score_grad = (probs * (prob_grad - row_dot) * SCALE).astype(jnp.bfloat16)
    return jnp.dot(score_grad, key_rows, preferred_element_type=jnp.float32).astype(jnp.bfloat16)


def routed(tokens_in, queries, key_value, out_grad, cluster_of, slot_of):
    groups = lax.axis_size("seq")
    tok_count = queries.shape[0]
    row_count = tok_count * H
    bound_rows = 2 * row_count // groups
    slot_count = CL_DEV * HALF
    owners = (cluster_of // CL_DEV).reshape(row_count)
    local_slot = (cluster_of % CL_DEV * HALF + slot_of % HALF).reshape(row_count)
    picked = (owners[:, None] == jnp.arange(groups, dtype=jnp.int32)[None, :]).astype(jnp.int32)
    ranked = jnp.sum(jnp.cumsum(picked, axis=0) * picked, axis=1) - 1
    cell_index = owners * bound_rows + ranked
    paired_rows = jnp.concatenate(
        [queries.reshape(row_count, HD), out_grad.reshape(row_count, HD)], axis=1
    )
    packed = jnp.concatenate([paired_rows, jnp.repeat(key_value, H, axis=0)], axis=1)
    outgoing = jnp.zeros((groups * bound_rows, 4 * HD), jnp.bfloat16).at[cell_index].set(packed)
    labels = jnp.full((groups * bound_rows,), -1, jnp.int32).at[cell_index].set(local_slot)
    incoming = lax.all_to_all(
        outgoing.reshape(groups, bound_rows, 4 * HD), "seq", 0, 0, tiled=True
    )
    labels_in = lax.all_to_all(labels.reshape(groups, bound_rows), "seq", 0, 0, tiled=True)
    target = labels_in.reshape(groups * bound_rows)
    target_safe = jnp.where(target >= 0, target, slot_count)
    arranged = (
        jnp.zeros((slot_count, 4 * HD), jnp.bfloat16)
        .at[target_safe]
        .set(incoming.reshape(groups * bound_rows, 4 * HD), mode="drop")
    )
    live_slot = (
        jnp.zeros((slot_count,), jnp.bfloat16)
        .at[target_safe]
        .set(jnp.ones((groups * bound_rows,), jnp.bfloat16), mode="drop")
    )
    arranged = arranged.reshape(CL_DEV, HALF, 4 * HD)
    keys_all = lax.all_gather(arranged[:, :, 2 * HD :], "pair", axis=1, tiled=True)
    live_all = lax.all_gather(live_slot.reshape(CL_DEV, HALF), "pair", axis=1, tiled=True)
    cluster_grads = lax.map(
        lambda ops: cluster_grad(*ops), (arranged[:, :, : 2 * HD], keys_all, live_all)
    )
    slot_grads = cluster_grads.reshape(slot_count, HD)
    going_back = jnp.where(
        target[:, None] >= 0,
        slot_grads[jnp.minimum(target_safe, slot_count - 1)],
        jnp.zeros((), jnp.bfloat16),
    )
    returned = lax.all_to_all(
        going_back.reshape(groups, bound_rows // 2, 2 * HD), "seq", 0, 0, tiled=True
    )
    query_grad = returned.reshape(groups * bound_rows, HD)[cell_index].reshape(tok_count, H * HD)
    partial_rows = lax.psum_scatter(
        lax.dot_general(
            tokens_in, query_grad, (((0,), (0,)), ((), ())), preferred_element_type=jnp.float32
        ),
        "seq",
        scatter_dimension=0,
        tiled=True,
    )
    return lax.psum_scatter(partial_rows, "pair", scatter_dimension=0, tiled=True)


def solution(mesh):
    n = mesh.shape["seq"]
    small = n * CL_DEV == 2 * HD and n & (n - 1) == 0
    spec = P(("seq", "pair"), None)
    return jax.shard_map(
        dense if small else routed,
        mesh=mesh,
        in_specs=(spec,) * 6,
        out_specs=spec,
        check_vma=False,
    )
```

```python
import jax
import jax.numpy as jnp
from jax import lax
from jax.experimental import pallas as pl
from jax.experimental.pallas import tpu as pltpu
from jax.sharding import PartitionSpec as P


H = 16
HD = 64
HALF = 512
CL_DEV = 8
SCALE = HD ** (-0.5)
TILE = 512
LAG = 1
LATE = 0.5
UNITS = 8


def prepare_rows_kernel(q_ref, g_ref, cl_ref, left, grd):
    tok, width = q_ref.shape
    lanes = 2 * HD
    ids = lax.broadcasted_iota(jnp.int32, (lanes, tok), 0)
    for i in range(width // lanes):
        two = slice(i * lanes, (i + 1) * lanes)
        qt = (q_ref[:, two].astype(jnp.float32) * SCALE).T.astype(jnp.bfloat16)
        gt = g_ref[:, two].astype(jnp.float32).T.astype(jnp.bfloat16)
        for odd in range(2):
            h = 2 * i + odd
            half = slice(odd * HD, (odd + 1) * HD)
            mine = cl_ref[h : h + 1, :]
            hot = jnp.where(ids == mine, 1.0, 0.0).astype(jnp.bfloat16)
            same = jnp.where(ids[:HD] == jnp.bitwise_and(mine, HD - 1), 1.0, 0.0)
            left[h, 0:HD, :] = qt[half]
            left[h, HD : HD + lanes, :] = hot
            left[h, HD + lanes :, :] = same.astype(jnp.bfloat16)
            grd[h, 0:HD, :] = jnp.zeros((HD, tok), jnp.bfloat16)
            grd[h, HD:, :] = gt[half]


def prepare_rows(queries, out_grad, cluster_of):
    tok, width = queries.shape
    heads = width // HD
    return pl.pallas_call(
        prepare_rows_kernel,
        out_shape=(
            jax.ShapeDtypeStruct((heads, 4 * HD, tok), jnp.bfloat16),
            jax.ShapeDtypeStruct((heads, 2 * HD, tok), jnp.bfloat16),
        ),
        compiler_params=pltpu.CompilerParams(vmem_limit_bytes=8 * 1024 * 1024),
        cost_estimate=pl.CostEstimate(flops=10**7, bytes_accessed=2 * 10**6, transcendentals=0),
    )(queries, out_grad, cluster_of.T)


def prepare_keys_kernel(*refs):
    kv_refs = refs[:-3]
    wide, key, turned = refs[-3:]
    tok = turned.shape[2]
    lanes = 2 * HD
    quarter = HD // 2
    ids = lax.broadcasted_iota(jnp.int32, (quarter, tok), 0)
    low = lax.broadcasted_iota(jnp.int32, (tok, lanes), 1) < HD
    at = 0
    for kv_ref in kv_refs:
        for j in range(kv_ref.shape[0]):
            rows = slice(at * tok, (at + 1) * tok)
            kv = kv_ref[j, 0:tok, :]
            kv32 = kv.astype(jnp.float32)
            key[rows, :] = kv
            turned[at, :, :] = kv32.T[:HD].astype(jnp.bfloat16)
            cl = kv_ref[j, tok : tok + H, :].astype(jnp.float32).astype(jnp.int32)
            group = jnp.bitwise_and(cl, quarter - 1)
            one = jnp.left_shift(1, 8 * jnp.right_shift(cl, 5))
            packed = jnp.zeros((quarter, tok), jnp.int32)
            for h in range(H):
                packed += jnp.where(group[h : h + 1, :] == ids, one[h : h + 1, :], 0)
            res, high = [], []
            for part in range(4):
                count = jnp.bitwise_and(jnp.right_shift(packed, 8 * part), 255)
                log = jnp.maximum(jnp.log(count.astype(jnp.float32)), -(2.0**100))
                hi = log.astype(jnp.bfloat16).astype(jnp.float32)
                high.append(hi)
                res.append(log - hi)
            small = []
            for part in range(2):
                a, b = res[part], res[part + 2]
                small.append(jnp.where(a == 0.0, b, jnp.where(b == 0.0, a, 0.5 * (a + b))))
            one = jnp.concatenate([high[0], high[1], high[0], high[1]], axis=0).T
            two = jnp.concatenate([high[2], high[3], small[0], small[1]], axis=0).T
            wide[0, rows, :] = jnp.where(low, kv32, one).astype(jnp.bfloat16)
            wide[1, rows, :] = two.astype(jnp.bfloat16)
            at += 1


def prepare_keys(gathered):
    tok = gathered[0].shape[2]
    blocks = sum(g.shape[0] for g in gathered)
    return pl.pallas_call(
        prepare_keys_kernel,
        out_shape=(
            jax.ShapeDtypeStruct((2, blocks * tok, 2 * HD), jnp.bfloat16),
            jax.ShapeDtypeStruct((blocks * tok, 2 * HD), jnp.bfloat16),
            jax.ShapeDtypeStruct((blocks, HD, tok), jnp.bfloat16),
        ),
        compiler_params=pltpu.CompilerParams(vmem_limit_bytes=8 * 1024 * 1024),
        cost_estimate=pl.CostEstimate(
            flops=blocks * 10**6, bytes_accessed=blocks * 10**5, transcendentals=0
        ),
    )(*gathered)


def attend_kernel(left, grd, *refs):
    count = (len(refs) - 10) // 3
    groups = [refs[3 * i : 3 * i + 3] for i in range(count)]
    out_ref, sc0, sc1, pg0, pg1, ds0, ds1, tp0, tp1, acc = refs[3 * count :]
    sc, pg, ds, tp = (sc0, sc1), (pg0, pg1), (ds0, ds1), (tp0, tp1)
    lanes = 2 * HD
    tok = out_ref.shape[0]
    rows = sc0.shape[1]
    per = TILE // tok
    places = [(g, j) for g, group in enumerate(groups) for j in range(group[2].shape[0] // per)]
    tiles = len(places)
    steps = out_ref.shape[1] // lanes
    unit = TILE // UNITS
    spread = (unit // 8, 8, rows)

    def tied(x, gate):
        if gate is None:
            return x
        tie = jnp.tile((gate * 0.0).astype(x.dtype), (1, x.shape[1] // gate.shape[1]))
        return jnp.concatenate([x[0:16] + tie, x[16:]], axis=0)

    def score(step, slot, t, gate):
        g, j = places[t]
        span = slice(j * TILE, (j + 1) * TILE)
        at = slice(t * TILE, (t + 1) * TILE)
        right = jnp.concatenate([left[2 * step], left[2 * step + 1]], axis=1)
        wide = jnp.concatenate([groups[g][0][0, span, :], groups[g][0][1, span, :]], axis=1)
        s = jnp.dot(wide, tied(right, gate), preferred_element_type=jnp.float32)
        sc[slot][at, :] = s
        top = jnp.max(s.reshape(TILE // 8, 8, rows), axis=0)
        tp[slot][...] = top if t == 0 else jnp.maximum(tp[slot][...], top)
        right = jnp.concatenate([grd[2 * step], grd[2 * step + 1]], axis=1)
        pg[slot][at, :] = jnp.dot(
            groups[g][1][span, :], tied(right, gate), preferred_element_type=jnp.float32
        )

    def collect(slot, t, gate):
        g, j = places[t]
        at = slice(t * TILE, (t + 1) * TILE)
        turned = jnp.concatenate([groups[g][2][j * per + b] for b in range(per)], axis=1)
        right = jnp.concatenate([ds[slot][0, at, :], ds[slot][1, at, :]], axis=1)
        add = jnp.dot(turned, tied(right, gate), preferred_element_type=jnp.float32)
        acc[...] = add if t == 0 else acc[...] + add

    def weigh(slot, u, top):
        at = slice(u * unit, (u + 1) * unit)
        w = jnp.exp(sc[slot][at, :].reshape(spread) - top)
        sc[slot][at, :] = w.reshape(unit, rows)
        wp = w * pg[slot][at, :].reshape(spread)
        return jnp.sum(w, axis=0), jnp.sum(wp, axis=0)

    def differ(slot, u, inv, dot):
        at = slice(u * unit, (u + 1) * unit)
        w = sc[slot][at, :].reshape(spread)
        d = (w * inv) * (pg[slot][at, :].reshape(spread) - dot)
        d = d.reshape(unit, rows)
        low = d.astype(jnp.bfloat16)
        for b in range(rows // lanes):
            ds[slot][b, at, :] = low[:, b * lanes : (b + 1) * lanes]
        return d[0:8, 0:lanes]

    def finish(step):
        both = jnp.concatenate([acc[:, b * lanes : (b + 1) * lanes] for b in range(2)], axis=0)
        where = pl.multiple_of(step * lanes, lanes)
        out_ref[:, pl.ds(where, lanes)] = both.T.astype(jnp.bfloat16)

    def stage(step, slot, following):
        units = tiles * UNITS
        work = [("w", u) for u in range(units)] + [("d", u) for u in range(units)]
        cost = [6.0 if kind == "w" else 4.0 for kind, _ in work]
        top = jnp.broadcast_to(jnp.max(tp[slot][...], axis=0, keepdims=True), (8, rows))[None]
        denom = jnp.zeros((8, rows), jnp.float32)
        dots = jnp.zeros((8, rows), jnp.float32)
        inv = dot = None
        gates, done, at = [None] * LAG, 0.0, 0
        for t in range(tiles):
            score(following, 1 - slot, t, gates[t])
            collect(1 - slot, t, gates[t])
            gate = None
            while at < len(work) and (t + 1 == tiles or done < sum(cost) * (t + 1) / (tiles + LATE)):
                kind, u = work[at]
                if kind == "w":
                    a, b = weigh(slot, u, top)
                    denom, dots = denom + a, dots + b
                    gate = denom[:, :lanes]
                else:
                    if inv is None:
                        whole = jnp.sum(denom, axis=0, keepdims=True)
                        dot = jnp.sum(dots, axis=0, keepdims=True) / whole
                        inv = jnp.broadcast_to(SCALE / whole, (8, rows))[None]
                        dot = jnp.broadcast_to(dot, (8, rows))[None]
                    one = differ(slot, u, inv, dot)
                    gate = one if gate is None else gate + one
                done += cost[at]
                at += 1
            gates.append(jnp.concatenate([gate, gate], axis=0))

        @pl.when(step > 0)
        def _():
            finish(step - 1)

    for t in range(tiles):
        score(0, 0, t, None)

    def body(i, _):
        stage(2 * i, 0, 2 * i + 1)
        stage(2 * i + 1, 1, jnp.minimum(2 * i + 2, steps - 1))
        return 0

    lax.fori_loop(0, steps // 2, body, 0)
    for t in range(tiles):
        collect(1, t, None)
    finish(steps - 1)


def attend(rows_of, groups, tok):
    left, grd = rows_of
    heads = left.shape[0]
    total = sum(g[1].shape[0] for g in groups)
    lanes = 2 * HD
    rows = 2 * tok
    operands = [left, grd] + [x for g in groups for x in g]
    work = heads * tok * total
    return pl.pallas_call(
        attend_kernel,
        in_specs=[pl.BlockSpec(memory_space=pltpu.VMEM)] * len(operands),
        out_specs=pl.BlockSpec(memory_space=pltpu.VMEM),
        out_shape=jax.ShapeDtypeStruct((tok, heads * HD), jnp.bfloat16),
        scratch_shapes=[pltpu.VMEM((total, rows), jnp.float32)] * 4
        + [pltpu.VMEM((rows // lanes, total, lanes), jnp.bfloat16)] * 2
        + [pltpu.VMEM((8, rows), jnp.float32)] * 2
        + [pltpu.VMEM((HD, rows), jnp.float32)],
        compiler_params=pltpu.CompilerParams(vmem_limit_bytes=40 * 1024 * 1024),
        cost_estimate=pl.CostEstimate(
            flops=work * 6 * HD, bytes_accessed=10**7, transcendentals=work
        ),
    )(*operands)


def xor_permute(x, axis, mask):
    n = lax.axis_size(axis)
    return lax.ppermute(x, axis, [(i, i ^ mask) for i in range(n)])


def dense(tokens_in, queries, key_value, out_grad, cluster_of, slot_of):
    n = lax.axis_size("seq")
    tok, width = queries.shape
    depth = tokens_in.shape[1]
    me = lax.axis_index("pair")
    low = 1
    while low * low < n:
        low *= 2
    high = n // low
    part, layer = lax.axis_index("seq") % low, lax.axis_index("seq") // low
    piece = depth // (2 * n)
    tie = lax.optimization_barrier

    own = jnp.concatenate([key_value, cluster_of.T.astype(jnp.bfloat16)], axis=0)[None]
    above = [xor_permute(own, "seq", low * k) for k in range(1, high)]
    left = prepare_rows(queries, out_grad, cluster_of)
    x5 = tokens_in.reshape(tok, high, low, 2, piece).transpose(2, 3, 0, 1, 4)
    x5 = x5.reshape(low, 2, tok, high * piece)
    above[-1], left, x5 = tie((above[-1], left, x5))
    column = jnp.concatenate([own] + above)
    near = [xor_permute(column, "seq", k) for k in range(1, low)]
    first = prepare_keys([column])
    near[-1], first = tie((near[-1], first))
    far = [xor_permute(p, "pair", 1) for p in [column] + near]
    second = prepare_keys(near)
    far[-1], second = tie((far[-1], second))
    groups = [first, second, prepare_keys(far)]

    x_part = [lax.dynamic_index_in_dim(x5, part ^ k, 0, keepdims=False) for k in range(low)]
    x_part = [x_part[0]] + [xor_permute(x_part[k], "seq", k) for k in range(1, low)]
    x_part = jnp.stack(x_part)
    x_mine = lax.dynamic_index_in_dim(x_part, me, 1, keepdims=False)
    x_pair = lax.dynamic_index_in_dim(x_part, 1 - me, 1, keepdims=False)
    x_pair = xor_permute(x_pair, "pair", 1)

    mine = attend(left, groups, tok)

    def product(x, grad):
        return lax.dot_general(
            x, grad, (((0,), (0,)), ((), ())), preferred_element_type=jnp.float32
        )

    grads = [mine] + [xor_permute(mine, "seq", k) for k in range(1, low)]
    pairs = [xor_permute(mine, "pair", 1)]
    block = product(x_mine[0], mine) + product(x_pair[0], pairs[0])
    grads[1], block = tie((grads[1], block))
    pairs += [xor_permute(g, "pair", 1) for g in grads[1:]]
    for k in range(1, low):
        block = block + product(x_mine[k], grads[k])
    for k in range(1, low):
        block = block + product(x_pair[k], pairs[k])
    block = block.reshape(high, piece, width)
    total = lax.dynamic_index_in_dim(block, layer, 0, keepdims=False)
    sent = block.astype(jnp.bfloat16)
    for k in range(1, high):
        term = lax.dynamic_index_in_dim(sent, layer ^ k, 0, keepdims=False)
        total = total + xor_permute(term, "seq", low * k).astype(jnp.float32)
    return total


def cluster_grad(query_part, key_part, live_keys):
    query_rows = query_part[:, :HD]
    grad_rows = query_part[:, HD:]
    key_rows = key_part[:, :HD]
    value_rows = key_part[:, HD:]
    scores = jnp.dot(query_rows, key_rows.T, preferred_element_type=jnp.float32) * SCALE
    scores = jnp.where(live_keys[None, :] > 0, scores, jnp.float32(-1e30))
    row_max = jnp.max(scores, axis=1, keepdims=True)
    weights = jnp.exp(scores - row_max)
    probs = weights / jnp.sum(weights, axis=1, keepdims=True)
    prob_grad = jnp.dot(grad_rows, value_rows.T, preferred_element_type=jnp.float32)
    row_dot = jnp.sum(probs * prob_grad, axis=1, keepdims=True)
    score_grad = (probs * (prob_grad - row_dot) * SCALE).astype(jnp.bfloat16)
    return jnp.dot(score_grad, key_rows, preferred_element_type=jnp.float32).astype(jnp.bfloat16)


def routed(tokens_in, queries, key_value, out_grad, cluster_of, slot_of):
    groups = lax.axis_size("seq")
    tok_count = queries.shape[0]
    row_count = tok_count * H
    bound_rows = 2 * row_count // groups
    slot_count = CL_DEV * HALF
    owners = (cluster_of // CL_DEV).reshape(row_count)
    local_slot = (cluster_of % CL_DEV * HALF + slot_of % HALF).reshape(row_count)
    picked = (owners[:, None] == jnp.arange(groups, dtype=jnp.int32)[None, :]).astype(jnp.int32)
    ranked = jnp.sum(jnp.cumsum(picked, axis=0) * picked, axis=1) - 1
    cell_index = owners * bound_rows + ranked
    paired_rows = jnp.concatenate(
        [queries.reshape(row_count, HD), out_grad.reshape(row_count, HD)], axis=1
    )
    packed = jnp.concatenate([paired_rows, jnp.repeat(key_value, H, axis=0)], axis=1)
    outgoing = jnp.zeros((groups * bound_rows, 4 * HD), jnp.bfloat16).at[cell_index].set(packed)
    labels = jnp.full((groups * bound_rows,), -1, jnp.int32).at[cell_index].set(local_slot)
    incoming = lax.all_to_all(
        outgoing.reshape(groups, bound_rows, 4 * HD), "seq", 0, 0, tiled=True
    )
    labels_in = lax.all_to_all(labels.reshape(groups, bound_rows), "seq", 0, 0, tiled=True)
    target = labels_in.reshape(groups * bound_rows)
    target_safe = jnp.where(target >= 0, target, slot_count)
    arranged = (
        jnp.zeros((slot_count, 4 * HD), jnp.bfloat16)
        .at[target_safe]
        .set(incoming.reshape(groups * bound_rows, 4 * HD), mode="drop")
    )
    live_slot = (
        jnp.zeros((slot_count,), jnp.bfloat16)
        .at[target_safe]
        .set(jnp.ones((groups * bound_rows,), jnp.bfloat16), mode="drop")
    )
    arranged = arranged.reshape(CL_DEV, HALF, 4 * HD)
    keys_all = lax.all_gather(arranged[:, :, 2 * HD :], "pair", axis=1, tiled=True)
    live_all = lax.all_gather(live_slot.reshape(CL_DEV, HALF), "pair", axis=1, tiled=True)
    cluster_grads = lax.map(
        lambda ops: cluster_grad(*ops), (arranged[:, :, : 2 * HD], keys_all, live_all)
    )
    slot_grads = cluster_grads.reshape(slot_count, HD)
    going_back = jnp.where(
        target[:, None] >= 0,
        slot_grads[jnp.minimum(target_safe, slot_count - 1)],
        jnp.zeros((), jnp.bfloat16),
    )
    returned = lax.all_to_all(
        going_back.reshape(groups, bound_rows // 2, 2 * HD), "seq", 0, 0, tiled=True
    )
    query_grad = returned.reshape(groups * bound_rows, HD)[cell_index].reshape(tok_count, H * HD)
    partial_rows = lax.psum_scatter(
        lax.dot_general(
            tokens_in, query_grad, (((0,), (0,)), ((), ())), preferred_element_type=jnp.float32
        ),
        "seq",
        scatter_dimension=0,
        tiled=True,
    )
    return lax.psum_scatter(partial_rows, "pair", scatter_dimension=0, tiled=True)


def solution(mesh):
    n = mesh.shape["seq"]
    small = n * CL_DEV == 2 * HD and n & (n - 1) == 0
    spec = P(("seq", "pair"), None)
    return jax.shard_map(
        dense if small else routed,
        mesh=mesh,
        in_specs=(spec,) * 6,
        out_specs=spec,
        check_vma=False,
    )
```
